1024 devices in a mesh: panel: 2 (over core), rad: 32 (over y_lo, z), ang: 16 (over y_hi, x).
Axes of the slice: x: 4, y: 8 (y_hi: 4, y_lo: 2; y = y_hi * 2 + y_lo), z: 16, core: 2. Of those that a mesh axis runs over, the one named last changes fastest.
Arguments:
- state: float32 [2, 6, 128, 64, 384], P('panel', None, 'rad', 'ang'), may hold values from 0.25 to 4
- velocity: float32 [2, 3, 128, 64, 384], P('panel', None, 'rad', 'ang'), may hold values from -1 to 1
- band_donor: int32 [2, 1792], replicated, may hold values from 770 to 23420, as said below
- band_weight: float32 [2, 4, 1792], replicated, may hold values from 0 to 1, as said below
Outputs:
- updated: float32 [2, 6, 128, 64, 384], P('panel', None, 'rad', 'ang')
The draws below stay inside these ranges and needn't reach their ends.
Inputs may be any that keep to these rules, and one draw needn't show every extreme that they name: band_donor[p, t] = row * 384 + col names the donor cells (row, col), (row, col + 1), (row + 1, col), (row + 1, col + 1) in the panel other than p, with row from 2 to 60 and col from 2 to 380. `band_weight`: the four weights of a zone are products of two factors in [0, 1], in the order of the donor cells, and sum to 1.
All inputs are finite; a program needn't handle non-finite values.
Results may differ from the reference program's by a relative error of at most 0.0003.
Values sent between devices are 32-bit elements; how exact they have to be, the bound alone decides.
A program may use at most 64 MiB of HBM per device.

```python
import math
import jax
import jax.numpy as jnp
from jax import lax

F = 6
G = 2
NPH = 384
NR = 128
NTH = 64
ZONES = 1792


def draw_band_donor(key, part):
    rows = jax.random.randint(jax.random.fold_in(key, 11), (2, ZONES), G, NTH - G - 1)
    columns = jax.random.randint(jax.random.fold_in(key, 12), (2, ZONES), G, NPH - G - 1)
    donor_cell = rows * NPH + columns
    lowest_place = jax.random.randint(jax.random.fold_in(key, 13), (2, 1), 0, ZONES)
    highest_place = (lowest_place + 1 + jax.random.randint(jax.random.fold_in(key, 14), (2, 1), 0, ZONES - 1)) % ZONES
    places = jnp.arange(ZONES)[None, :]
    donor_cell = jnp.where(places == lowest_place, G * NPH + G, donor_cell)
    donor_cell = jnp.where(places == highest_place, (NTH - G - 2) * NPH + NPH - G - 2, donor_cell)
    return donor_cell.astype(jnp.int32)


def draw_band_weight(key, part):
    across = jax.random.uniform(jax.random.fold_in(key, 21), (2, ZONES), jnp.float32)
    sideways = jax.random.uniform(jax.random.fold_in(key, 22), (2, ZONES), jnp.float32)
    return jnp.stack([(1.0 - across) * (1.0 - sideways), (1.0 - across) * sideways, across * (1.0 - sideways), across * sideways], axis=1).astype(jnp.float32)


def block_levels(stream_key, dims, cuts, smallest, largest):
    factor_of, own = 1.0, jax.random.fold_in(stream_key, 6)
    for position, blocks in cuts:
        steps = jnp.exp(jax.random.uniform(jax.random.fold_in(own, position), (blocks,), jnp.float32, smallest / len(cuts), largest / len(cuts)))
        factor_of = factor_of * jnp.repeat(steps, dims[position] // blocks).reshape([-1 if axis == position else 1 for axis in range(len(dims))])
    return factor_of


def setup_inputs(seed: int = 0) -> dict:
    key_list = jax.random.split(jax.random.key(seed), 5)
    return {
        "state": jnp.clip(jnp.exp(math.log(4.0) - 2.7725887 * jax.random.uniform(key_list[0], (2, F, NR, NTH, NPH), jnp.float32) ** block_levels(key_list[0], (2, F, NR, NTH, NPH), ((0, 2), (2, 32), (3, 16)), -0.2, 0.2)), 0.25, 4.0),
        "velocity": jnp.clip(jax.random.uniform(key_list[1], (2, 3, NR, NTH, NPH), jnp.float32, -1.0, 1.0) * block_levels(key_list[1], (2, 3, NR, NTH, NPH), ((0, 2), (2, 32), (3, 16)), -0.4, 0.0), -1.0, 1.0),
        "band_donor": draw_band_donor(jax.random.fold_in(key_list[4], 71), 0),
        "band_weight": draw_band_weight(jax.random.fold_in(key_list[4], 71), 0),
    }


inner_radius = 1.0
courant_limit = 0.8


def geometry(theta_cells, phi_cells):
    theta_step = (math.pi / 2) / (theta_cells - 2 * G)
    phi_step = (1.5 * math.pi) / (phi_cells - 2 * G)
    radius_step = inner_radius * theta_step
    theta_start = math.pi / 4 - G * theta_step
    time_step = courant_limit * inner_radius * min(theta_step, math.sin(theta_start) * phi_step)
    return theta_step, phi_step, radius_step, theta_start, time_step


def window(values, first_cell, how_many, direction):
    return lax.slice_in_dim(values, first_cell, first_cell + how_many, axis=direction)


def transport(values, motion, direction, face_area, face_rate, cell_rate):
    cells = values.shape[direction] - 6
    left_cells = window(values, 1, cells + 3, direction)
    right_cells = window(values, 2, cells + 3, direction)
    interface = (7.0 / 12.0) * (left_cells + right_cells) - (1.0 / 12.0) * (window(values, 0, cells + 3, direction) + window(values, 3, cells + 3, direction))
    interface = jnp.clip(interface, jnp.minimum(left_cells, right_cells), jnp.maximum(left_cells, right_cells))
    left_edge = window(interface, 0, cells + 2, direction)
    right_edge = window(interface, 1, cells + 2, direction)
    middle = window(values, 2, cells + 2, direction)
    spread = right_edge - left_edge
    curvature = 6.0 * (middle - 0.5 * (left_edge + right_edge))
    face_speed = 0.5 * (window(motion, 2, cells + 1, direction) + window(motion, 3, cells + 1, direction))
    courant = jnp.abs(face_speed) * face_rate
    keeping = 1.0 - (2.0 / 3.0) * courant
    from_left = window(right_edge, 0, cells + 1, direction) - 0.5 * courant * (window(spread, 0, cells + 1, direction) - keeping * window(curvature, 0, cells + 1, direction))
    from_right = window(left_edge, 1, cells + 1, direction) + 0.5 * courant * (window(spread, 1, cells + 1, direction) + keeping * window(curvature, 1, cells + 1, direction))
    face_flux = face_area * face_speed * jnp.where(face_speed > 0, from_left, from_right)
    return window(values, 3, cells, direction) - cell_rate * (window(face_flux, 1, cells, direction) - window(face_flux, 0, cells, direction))


def edge_pad(values, direction):
    widths = [(0, 0)] * values.ndim
    widths[direction] = (3, 3)
    return jnp.pad(values, widths, mode="edge")


def reference(state, velocity, band_donor, band_weight):
    theta_step, phi_step, radius_step, theta_start, time_step = geometry(NTH, NPH)
    radius_face = inner_radius + jnp.arange(NR + 1, dtype=jnp.float32) * radius_step
    radius_cell = inner_radius + (jnp.arange(NR, dtype=jnp.float32) + 0.5) * radius_step
    theta_face = theta_start + jnp.arange(NTH + 1, dtype=jnp.float32) * theta_step
    theta_cell = theta_start + (jnp.arange(NTH, dtype=jnp.float32) + 0.5) * theta_step
    radial_area = (radius_face * radius_face)[:, None, None]
    radial_step = time_step / radius_step
    radial_rate = (time_step / (radius_cell * radius_cell * radius_step))[:, None, None]
    polar_area = jnp.sin(theta_face)[None, :, None]
    polar_step = (time_step / (radius_cell * theta_step))[:, None, None]
    polar_rate = (time_step / (radius_cell[:, None] * jnp.sin(theta_cell)[None, :] * theta_step))[:, :, None]
    azimuth_rate = (time_step / (radius_cell[:, None] * jnp.sin(theta_cell)[None, :] * phi_step))[:, :, None]
    after_sweeps = []
    for panel_index in range(2):
        motion = velocity[panel_index]
        radial_motion = edge_pad(motion[0], 0)
        polar_motion = edge_pad(motion[1], 1)
        azimuth_motion = edge_pad(motion[2], 2)
        fields = []
        for field_index in range(F):
            values = state[panel_index, field_index]
            values = transport(edge_pad(values, 0), radial_motion, 0, radial_area, radial_step, radial_rate)
            values = transport(edge_pad(values, 1), polar_motion, 1, polar_area, polar_step, polar_rate)
            values = transport(edge_pad(values, 2), azimuth_motion, 2, 1.0, azimuth_rate, azimuth_rate)
            fields.append(values)
        after_sweeps.append(jnp.stack(fields))
    theta_rows = jnp.concatenate([jnp.arange(G), NTH - G + jnp.arange(G)]).astype(jnp.int32)
    theta_targets = (theta_rows[:, None] * NPH + jnp.arange(NPH)[None, :]).reshape(-1).astype(jnp.int32)
    phi_columns = jnp.concatenate([jnp.arange(G), NPH - G + jnp.arange(G)]).astype(jnp.int32)
    phi_targets = (jnp.arange(NTH)[:, None] * NPH + phi_columns[None, :]).reshape(-1).astype(jnp.int32)
    outputs = []
    for panel_index in range(2):
        twin_block = after_sweeps[1 - panel_index].reshape(F, NR, NTH * NPH)
        donor_cell = band_donor[panel_index].astype(jnp.int32)
        weights = band_weight[panel_index]
        band_values = weights[0] * jnp.take(twin_block, donor_cell, axis=2)
        band_values = band_values + weights[1] * jnp.take(twin_block, donor_cell + 1, axis=2)
        band_values = band_values + weights[2] * jnp.take(twin_block, donor_cell + NPH, axis=2)
        band_values = band_values + weights[3] * jnp.take(twin_block, donor_cell + NPH + 1, axis=2)
        flat_block = after_sweeps[panel_index].reshape(F, NR, NTH * NPH)
        flat_block = flat_block.at[:, :, phi_targets].set(band_values[:, :, 2 * G * NPH:])
        flat_block = flat_block.at[:, :, theta_targets].set(band_values[:, :, :2 * G * NPH])
        outputs.append(flat_block.reshape(F, NR, NTH, NPH))
    return jnp.stack(outputs)
```

```python
import functools
import math

import jax
import jax.numpy as jnp
from jax import lax
from jax.experimental import pallas as pl
from jax.experimental.pallas import tpu as pltpu
from jax.sharding import PartitionSpec as P

G = 2
INNER_RADIUS = 1.0
COURANT = 0.8
MESH = pl.DeviceIdType.MESH
F32 = jnp.float32
BF16 = jnp.bfloat16


def geometry(theta_cells, phi_cells):
    theta_step = math.pi / 2 / (theta_cells - 2 * G)
    phi_step = 1.5 * math.pi / (phi_cells - 2 * G)
    radius_step = INNER_RADIUS * theta_step
    theta_start = math.pi / 4 - G * theta_step
    time_step = COURANT * INNER_RADIUS * min(theta_step, math.sin(theta_start) * phi_step)
    return theta_step, phi_step, radius_step, theta_start, time_step


def flux_coefficients(face_speed, area, face_rate):
    size = jnp.abs(face_speed)
    courant = size * face_rate
    half = 0.5 * courant
    a0 = face_speed if area is None else area * face_speed
    a1 = a0 * (half * (1.0 - 2.0 / 3.0 * courant))
    a2 = -(half * (size if area is None else area * size))
    return a0, a1, a2


def clipped_interface(before, left, right, after):
    value = 7.0 / 12.0 * (left + right) - 1.0 / 12.0 * (before + after)
    return jnp.minimum(jnp.maximum(value, jnp.minimum(left, right)), jnp.maximum(left, right))


def sweep_leading(q, a0, a1, a2, rate):
    n = q.shape[0] - 6
    face = clipped_interface(q[0 : n + 3], q[1 : n + 4], q[2 : n + 5], q[3 : n + 6])
    left, right = face[0 : n + 2], face[1 : n + 3]
    spread = right - left
    curvature = 6.0 * (q[2 : n + 4] - 0.5 * (left + right))
    up = a0 > 0
    flux = (
        a0 * face[1 : n + 2]
        + a1 * jnp.where(up, curvature[0 : n + 1], curvature[1 : n + 2])
        + a2 * jnp.where(up, spread[0 : n + 1], spread[1 : n + 2])
    )
    return q[3 : n + 3] - rate * (flux[1 : n + 1] - flux[0:n])


def with_ghost_lanes(x):
    rows, cells = x.shape
    lane = lax.broadcasted_iota(jnp.int32, (rows, 128), 1)
    last = jnp.broadcast_to(x[:, cells - 1 : cells], (rows, 128))
    first = jnp.broadcast_to(x[:, 0:1], (rows, 128))
    return jnp.concatenate([x, jnp.where(lane < 64, last, first)], axis=1)


def sweep_lanes(q, a0, a1, a2, rate):
    width = q.shape[1]
    cells = width - 128
    before = pltpu.roll(q, 1, 1)
    face = clipped_interface(pltpu.roll(q, 2, 1), before, q, pltpu.roll(q, width - 1, 1))
    right = pltpu.roll(face, width - 1, 1)
    spread = right - face
    curvature = 6.0 * (q - 0.5 * (face + right))
    up = a0 > 0
    flux = (
        a0 * face
        + a1 * jnp.where(up, pltpu.roll(curvature, 1, 1), curvature)
        + a2 * jnp.where(up, pltpu.roll(spread, 1, 1), spread)
    )
    change = pltpu.roll(flux, width - 1, 1) - flux
    return q[:, :cells] - rate * change[:, :cells]


def put(ref, index, rows, value):
    for c in range(value.shape[1] // 128):
        ref[index, c, rows, :] = value[:, 128 * c : 128 * c + 128]


def get(ref, index, rows):
    return jnp.concatenate([ref[index, c, rows, :] for c in range(ref.shape[1])], axis=1)


def kernel(
    sizes,
    state_hbm,
    velocity_hbm,
    donor_ref,
    weight_ref,
    out_ref,
    own,
    vel,
    rad_ext,
    rad_vel,
    stage,
    ang_ext,
    ang_vel,
    azi_coef,
    swept,
    planes,
    split,
    onehot,
    near_weight,
    far_weight,
    zone_sum,
    theta_out,
    phi_out,
    theta_in,
    phi_in,
    phi_rows,
    local_sem,
    halo_send,
    halo_recv,
    plane_send,
    plane_recv,
    zone_send,
    theta_recv,
    phi_recv,
):
    n_rad, n_ang, groups, nr, nt, nphi, theta_cells, zones = sizes
    panel = lax.axis_index("panel")
    rad = lax.axis_index("rad")
    ang = lax.axis_index("ang")
    twin = 1 - panel
    theta_step, phi_step, radius_step, theta_start, time_step = geometry(theta_cells, nphi)
    first_owner = 2
    owners = groups * nr
    is_owner = (ang >= first_owner) & (ang < first_owner + owners)

    load_state = pltpu.make_async_copy(state_hbm, own, local_sem.at[0])
    load_velocity = pltpu.make_async_copy(velocity_hbm, vel, local_sem.at[1])
    load_state.start()
    load_velocity.start()

    rad_down = (panel, lax.rem(rad + n_rad - 1, n_rad), ang)
    rad_up = (panel, lax.rem(rad + 1, n_rad), ang)
    ang_down = (panel, rad, lax.rem(ang + n_ang - 1, n_ang))
    ang_up = (panel, rad, lax.rem(ang + 1, n_ang))

    barrier = pltpu.get_barrier_semaphore()
    pl.semaphore_signal(barrier, inc=1, device_id=rad_down, device_id_type=MESH)
    pl.semaphore_signal(barrier, inc=1, device_id=rad_up, device_id_type=MESH)
    members = 2 * n_ang
    place = panel * n_ang + ang

    def greet(k, carry):
        other = lax.rem(place + k, members)
        pl.semaphore_signal(
            barrier,
            inc=1,
            device_id=(other // n_ang, rad, lax.rem(other, n_ang)),
            device_id_type=MESH,
        )
        return carry

    lax.fori_loop(1, members, greet, 0)

    load_state.wait()
    load_velocity.wait()
    for g in range(groups):
        for f in range(2):
            for r in range(nr):
                rad_ext[g, 3 + r, f * nt : (f + 1) * nt, :] = own[2 * g + f, r]
    for r in range(nr):
        for f in range(2):
            rad_vel[1 + r, f * nt : (f + 1) * nt, :] = vel[0, r]
            row = (2 * r + f) * nt
            put(stage, groups, pl.ds(row, nt), vel[1, r])
            put(stage, groups + 1, pl.ds(row, nt), vel[2, r])
    for t in range(nt):
        ang_vel[1 + t] = get(stage, groups, pl.ds(t, 2 * nr, stride=nt))

    pl.semaphore_wait(barrier, members + 1)

    def send(src, dst, slot, device):
        return pltpu.make_async_remote_copy(
            src_ref=src,
            dst_ref=dst,
            send_sem=halo_send.at[slot],
            recv_sem=halo_recv.at[slot],
            device_id=device,
            device_id_type=MESH,
        )

    rad_copies, ang_copies = [], []
    for g in range(groups):
        rad_copies.append(
            (
                send(rad_ext.at[g, 3:6], rad_ext.at[g, nr + 3 : nr + 6], 4 * g, rad_down),
                send(rad_ext.at[g, nr : nr + 3], rad_ext.at[g, 0:3], 4 * g + 1, rad_up),
            )
        )
        ang_copies.append(
            (
                send(ang_ext.at[g, 3:6], ang_ext.at[g, nt + 3 : nt + 6], 4 * g + 2, ang_down),
                send(ang_ext.at[g, nt : nt + 3], ang_ext.at[g, 0:3], 4 * g + 3, ang_up),
            )
        )
    base = 4 * groups
    rad_vel_copies = (
        send(rad_vel.at[1], rad_vel.at[nr + 1], base, rad_down),
        send(rad_vel.at[nr], rad_vel.at[0], base + 1, rad_up),
    )
    ang_vel_copies = (
        send(ang_vel.at[1], ang_vel.at[nt + 1], base + 2, ang_down),
        send(ang_vel.at[nt], ang_vel.at[0], base + 3, ang_up),
    )
    for copy in rad_vel_copies + rad_copies[0] + ang_vel_copies:
        copy.start()
    for g in range(1, groups):
        for copy in rad_copies[g]:
            copy.start()

    @pl.when(is_owner)
    def _():
        donor_all = donor_ref[...]
        donor = jnp.where(panel == 0, donor_all[1:2], donor_all[0:1]).astype(F32)
        donor_row = jnp.floor((donor + 0.5) * (1.0 / nphi))
        donor_col = donor - donor_row * nphi
        weights = jnp.where(panel == 0, weight_ref[1], weight_ref[0])
        cells = 2 * theta_cells
        row_of = lax.broadcasted_iota(jnp.int32, (cells, 128), 0)
        row_of = ((row_of // (2 * nt)) * nt + lax.rem(row_of, nt)).astype(F32)
        col_of = lax.broadcasted_iota(jnp.int32, (nphi, 128), 0).astype(F32)
        for z in range(0, zones, 128):
            here = donor_row[:, z : z + 128]
            w = weights[:, z : z + 128]
            at_row = row_of == here
            above = row_of == here + 1.0
            near_weight[:, z : z + 128] = jnp.where(
                at_row, w[0:1], jnp.where(above, w[2:3], 0.0)
            )
            far_weight[:, z : z + 128] = jnp.where(
                at_row, w[1:2], jnp.where(above, w[3:4], 0.0)
            )
            hot = jnp.where(col_of == donor_col[:, z : z + 128], 1.0, 0.0).astype(BF16)
            onehot[0:nphi, z : z + 128] = hot
            onehot[nphi : 2 * nphi, z : z + 128] = hot

    def wide(x, tiles):
        return jnp.concatenate([x] * tiles, axis=-1)

    tiles = nphi // 128
    lead = lambda n: lax.broadcasted_iota(jnp.int32, (n, 8, 128), 0)
    sub = lambda n: lax.broadcasted_iota(jnp.int32, (n, 8, 128), 1)
    radius_of_row = (
        INNER_RADIUS + ((rad * nr + sub(nt) // 2).astype(F32) + 0.5) * radius_step
    )
    theta_cell = theta_start + ((ang * nt + lead(nt)).astype(F32) + 0.5) * theta_step
    sin_cell = jnp.sin(theta_cell)
    polar_rate = wide(time_step / (radius_of_row * sin_cell * theta_step), tiles)
    azimuth_rate = time_step / (radius_of_row * sin_cell * phi_step)
    azimuth_rate = azimuth_rate.reshape(nt * 8, 128)
    azi_u = jnp.concatenate(
        [get(stage, groups + 1, pl.ds(t, 2 * nr, stride=nt)) for t in range(nt)], axis=0
    )
    azi_u = with_ghost_lanes(azi_u)
    azi_face = 0.5 * (azi_u + pltpu.roll(azi_u, 1, 1))
    for i, coefficient in enumerate(
        flux_coefficients(azi_face, None, wide(azimuth_rate, tiles + 1))
    ):
        azi_coef[i] = coefficient
    azimuth_rate = wide(azimuth_rate, tiles)

    for copy in rad_vel_copies:
        copy.wait_recv()
    v = rad_vel[...]
    v_first = jnp.where(rad == 0, v[1:2], v[0:1])
    v_last = jnp.where(rad == n_rad - 1, v[nr : nr + 1], v[nr + 1 : nr + 2])
    v = jnp.concatenate([v_first, v[1 : nr + 1], v_last], axis=0)
    radius_face = INNER_RADIUS + (rad * nr + lead(nr + 1)).astype(F32) * radius_step
    radius_cell = INNER_RADIUS + ((rad * nr + lead(nr)).astype(F32) + 0.5) * radius_step
    rad_coef = flux_coefficients(
        0.5 * (v[0 : nr + 1] + v[1 : nr + 2]),
        wide(radius_face * radius_face, tiles),
        time_step / radius_step,
    )
    rad_rate = wide(time_step / (radius_cell * radius_cell * radius_step), tiles)
    for g in range(groups):
        for copy in rad_copies[g]:
            copy.wait_recv()
        q = rad_ext[g]
        inner = q[3 : nr + 3]
        low = jnp.where(rad == 0, jnp.concatenate([inner[0:1]] * 3, axis=0), q[0:3])
        high = jnp.where(
            rad == n_rad - 1, jnp.concatenate([inner[nr - 1 : nr]] * 3, axis=0), q[nr + 3 : nr + 6]
        )
        after = sweep_leading(jnp.concatenate([low, inner, high], axis=0), *rad_coef, rad_rate)
        for r in range(nr):
            put(stage, g, pl.ds(8 * r, 8), after[r])
        for t in range(nt):
            ang_ext[g, 3 + t] = get(stage, g, pl.ds(t, 2 * nr, stride=nt))
        for copy in ang_copies[g]:
            copy.start()

    for copy in ang_vel_copies:
        copy.wait_recv()
    v = ang_vel[...]
    v_first = jnp.where(ang == 0, v[1:2], v[0:1])
    v_last = jnp.where(ang == n_ang - 1, v[nt : nt + 1], v[nt + 1 : nt + 2])
    v = jnp.concatenate([v_first, v[1 : nt + 1], v_last], axis=0)
    theta_face = theta_start + (ang * nt + lead(nt + 1)).astype(F32) * theta_step
    radius_of_face = INNER_RADIUS + ((rad * nr + sub(nt + 1) // 2).astype(F32) + 0.5) * radius_step
    ang_coef = flux_coefficients(
        0.5 * (v[0 : nt + 1] + v[1 : nt + 2]),
        wide(jnp.sin(theta_face), tiles),
        wide(time_step / (radius_of_face * theta_step), tiles),
    )

    def plane_copy(g, r):
        return pltpu.make_async_remote_copy(
            src_ref=swept.at[g, :, 8 * r : 8 * r + 8],
            dst_ref=planes.at[ang],
            send_sem=plane_send.at[g * nr + r],
            recv_sem=plane_recv,
            device_id=(panel, rad, first_owner + g * nr + r),
            device_id_type=MESH,
        )

    for g in range(groups):
        for copy in ang_copies[g]:
            copy.wait_recv()
        q = ang_ext[g]
        inner = q[3 : nt + 3]
        low = jnp.where(ang == 0, jnp.concatenate([inner[0:1]] * 3, axis=0), q[0:3])
        high = jnp.where(
            ang == n_ang - 1, jnp.concatenate([inner[nt - 1 : nt]] * 3, axis=0), q[nt + 3 : nt + 6]
        )
        polar = sweep_leading(jnp.concatenate([low, inner, high], axis=0), *ang_coef, polar_rate)
        cells = with_ghost_lanes(polar.reshape(nt * 8, nphi))
        done = sweep_lanes(cells, azi_coef[0], azi_coef[1], azi_coef[2], azimuth_rate)
        for t in range(nt):
            put(swept, g, pl.ds(t, 2 * nr, stride=nt), done[8 * t : 8 * t + 8])
        for r in range(nr):
            @pl.when(ang != first_owner + g * nr + r)
            def _():
                plane_copy(g, r).start()

            @pl.when(ang == first_owner + g * nr + r)
            def _():
                pltpu.make_async_copy(
                    swept.at[g, :, 8 * r : 8 * r + 8], planes.at[ang], plane_recv
                ).start()

    def zone_copies():
        order = ang - first_owner
        copies = []
        for side, target in ((0, 0), (1, n_ang - 1)):
            copies.append(
                pltpu.make_async_remote_copy(
                    src_ref=theta_out.at[side],
                    dst_ref=theta_in.at[order],
                    send_sem=zone_send.at[n_ang + side],
                    recv_sem=theta_recv,
                    device_id=(twin, rad, target),
                    device_id_type=MESH,
                )
            )
        for target in range(n_ang):
            copies.append(
                pltpu.make_async_remote_copy(
                    src_ref=phi_out.at[target // (n_ang // 2)],
                    dst_ref=phi_in.at[order],
                    send_sem=zone_send.at[target],
                    recv_sem=phi_recv,
                    device_id=(twin, rad, target),
                    device_id_type=MESH,
                )
            )
        return copies

    @pl.when(is_owner)
    def _():
        pltpu.make_async_copy(planes, planes, plane_recv).wait()
        cells = 2 * theta_cells
        x = jnp.concatenate(
            [planes[:, c].reshape(cells, 128) for c in range(nphi // 128)], axis=1
        )
        for i, part in enumerate((x, pltpu.roll(x, nphi - 1, 1))):
            high = part.astype(BF16)
            split[i * cells : (i + 1) * cells, 0:nphi] = high
            split[i * cells : (i + 1) * cells, nphi : 2 * nphi] = (
                part - high.astype(F32)
            ).astype(BF16)
        x = split[...]
        for z in range(0, zones, 256):
            y = jnp.dot(x, onehot[:, z : z + 256], preferred_element_type=F32)
            picked = (
                near_weight[:, z : z + 256] * y[:cells] + far_weight[:, z : z + 256] * y[cells:]
            )
            zone_sum[:, z : z + 256] = picked.reshape(n_ang, 2 * nt, 256).sum(axis=0)
        for f in range(2):
            line = jnp.sum(zone_sum[f * nt : (f + 1) * nt, :], axis=0, keepdims=True)
            for side in range(2):
                for row in range(G):
                    start = (side * G + row) * nphi
                    theta_out[side, row, f : f + 1, :] = line[:, start : start + nphi]
                start = 2 * G * nphi + side * 128
                phi_out[side, f : f + 1, :] = line[:, start : start + 128]
        for copy in zone_copies():
            copy.start()

    pltpu.make_async_copy(phi_in, phi_in, phi_recv).wait()
    for g in range(groups):
        for r in range(nr):
            @pl.when(ang != first_owner + g * nr + r)
            def _():
                plane_copy(g, r).wait_send()

    for o in range(owners):
        phi_rows[2 * o : 2 * o + 2, :] = phi_in[o]
    rows = phi_rows[...]
    lane = lax.broadcasted_iota(jnp.int32, (8, 128), 1)
    start = lax.rem(ang, n_ang // 2) * (2 * G * nt)
    for t in range(nt):
        left = pltpu.roll(rows, lax.rem(256 - start - 2 * G * t, 128), 1)
        right = pltpu.roll(rows, lax.rem(256 - start - 2 * G * t - 2 * G, 128), 1)
        for g in range(groups):
            line = get(swept, g, pl.ds(t, 2 * nr, stride=nt))
            line = jnp.concatenate(
                [
                    jnp.where(lane < G, left[8 * g : 8 * g + 8], line[:, :128]),
                    line[:, 128 : nphi - 128],
                    jnp.where(lane >= 128 - G, right[8 * g : 8 * g + 8], line[:, nphi - 128 :]),
                ],
                axis=1,
            )
            put(stage, g, pl.ds(t, 2 * nr, stride=nt), line)

    def fill_rows(first_row):
        pltpu.make_async_copy(theta_in, theta_in, theta_recv).wait()
        for row in range(G):
            for g in range(groups):
                for r in range(nr):
                    ang_ext[g, row, 2 * r : 2 * r + 2, :] = theta_in[g * nr + r, row]
                put(stage, g, pl.ds(first_row + row, 2 * nr, stride=nt), ang_ext[g, row])

    @pl.when(ang == 0)
    def _():
        fill_rows(0)

    @pl.when(ang == n_ang - 1)
    def _():
        fill_rows(nt - G)

    for g in range(groups):
        for f in range(2):
            for r in range(nr):
                row = (2 * r + f) * nt
                out_ref[2 * g + f, r] = get(stage, g, pl.ds(row, nt))

    for copy in rad_vel_copies + ang_vel_copies:
        copy.wait_send()
    for g in range(groups):
        for copy in rad_copies[g] + ang_copies[g]:
            copy.wait_send()

    @pl.when(is_owner)
    def _():
        for copy in zone_copies():
            copy.wait_send()


def solution(mesh):
    n_rad, n_ang = mesh.shape["rad"], mesh.shape["ang"]

    def body(state, velocity, band_donor, band_weight):
        _, fields, nr, nt, nphi = state.shape
        zones = band_donor.shape[1]
        groups = fields // 2
        owners = groups * nr
        theta_cells = nt * n_ang
        sizes = (n_rad, n_ang, groups, nr, nt, nphi, theta_cells, zones)
        n_halo = 4 * groups + 4
        out = pl.pallas_call(
            functools.partial(kernel, sizes),
            out_shape=jax.ShapeDtypeStruct((fields, nr, nt, nphi), F32),
            in_specs=[
                pl.BlockSpec(memory_space=pl.ANY),
                pl.BlockSpec(memory_space=pl.ANY),
                pl.BlockSpec(memory_space=pltpu.VMEM),
                pl.BlockSpec(memory_space=pltpu.VMEM),
            ],
            out_specs=pl.BlockSpec(memory_space=pltpu.VMEM),
            scratch_shapes=[
                pltpu.VMEM((fields, nr, nt, nphi), F32),
                pltpu.VMEM((3, nr, nt, nphi), F32),
                pltpu.VMEM((groups, nr + 6, 8, nphi), F32),
                pltpu.VMEM((nr + 2, 8, nphi), F32),
                pltpu.VMEM((groups + 2, nphi // 128, 8 * nr, 128), F32),
                pltpu.VMEM((groups, nt + 6, 8, nphi), F32),
                pltpu.VMEM((nt + 2, 8, nphi), F32),
                pltpu.VMEM((3, 8 * nt, nphi + 128), F32),
                pltpu.VMEM((groups, nphi // 128, 8 * nr, 128), F32),
                pltpu.VMEM((n_ang, nphi // 128, 2 * nt, 128), F32),
                pltpu.VMEM((4 * theta_cells, 2 * nphi), BF16),
                pltpu.VMEM((2 * nphi, zones), BF16),
                pltpu.VMEM((2 * theta_cells, zones), F32),
                pltpu.VMEM((2 * theta_cells, zones), F32),
                pltpu.VMEM((2 * nt, zones), F32),
                pltpu.VMEM((2, G, 2, nphi), F32),
                pltpu.VMEM((2, 2, 128), F32),
                pltpu.VMEM((owners, G, 2, nphi), F32),
                pltpu.VMEM((owners, 2, 128), F32),
                pltpu.VMEM((2 * owners, 128), F32),
                pltpu.SemaphoreType.DMA((2,)),
                pltpu.SemaphoreType.DMA((n_halo,)),
                pltpu.SemaphoreType.DMA((n_halo,)),
                pltpu.SemaphoreType.DMA((owners,)),
                pltpu.SemaphoreType.DMA,
                pltpu.SemaphoreType.DMA((n_ang + 2,)),
                pltpu.SemaphoreType.DMA,
                pltpu.SemaphoreType.DMA,
            ],
            compiler_params=pltpu.CompilerParams(
                collective_id=0, has_side_effects=True, vmem_limit_bytes=40 * 1024 * 1024
            ),
        )(state[0], velocity[0], band_donor, band_weight)
        return out[None]

    spec = P("panel", None, "rad", "ang", None)
    return jax.shard_map(
        body, mesh=mesh, in_specs=(spec, spec, P(), P()), out_specs=spec, check_vma=False
    )
```

```python
import functools
import math

import jax
import jax.numpy as jnp
from jax import lax
from jax.experimental import pallas as pl
from jax.experimental.pallas import tpu as pltpu
from jax.sharding import PartitionSpec as P

G = 2
INNER_RADIUS = 1.0
COURANT = 0.8
MESH = pl.DeviceIdType.MESH
F32 = jnp.float32
BF16 = jnp.bfloat16


def geometry(theta_cells, phi_cells):
    theta_step = math.pi / 2 / (theta_cells - 2 * G)
    phi_step = 1.5 * math.pi / (phi_cells - 2 * G)
    radius_step = INNER_RADIUS * theta_step
    theta_start = math.pi / 4 - G * theta_step
    time_step = COURANT * INNER_RADIUS * min(theta_step, math.sin(theta_start) * phi_step)
    return theta_step, phi_step, radius_step, theta_start, time_step


def flux_coefficients(face_speed, area, face_rate):
    size = jnp.abs(face_speed)
    courant = size * face_rate
    half = 0.5 * courant
    a0 = face_speed if area is None else area * face_speed
    a1 = a0 * (half * (1.0 - 2.0 / 3.0 * courant))
    a2 = -(half * (size if area is None else area * size))
    return a0, a1, a2


def clipped_interface(before, left, right, after):
    value = 7.0 / 12.0 * (left + right) - 1.0 / 12.0 * (before + after)
    return jnp.minimum(jnp.maximum(value, jnp.minimum(left, right)), jnp.maximum(left, right))


def sweep_leading(q, a0, a1, a2, rate):
    n = q.shape[0] - 6
    face = clipped_interface(q[0 : n + 3], q[1 : n + 4], q[2 : n + 5], q[3 : n + 6])
    left, right = face[0 : n + 2], face[1 : n + 3]
    spread = right - left
    curvature = 6.0 * (q[2 : n + 4] - 0.5 * (left + right))
    up = a0 > 0
    flux = (
        a0 * face[1 : n + 2]
        + a1 * jnp.where(up, curvature[0 : n + 1], curvature[1 : n + 2])
        + a2 * jnp.where(up, spread[0 : n + 1], spread[1 : n + 2])
    )
    return q[3 : n + 3] - rate * (flux[1 : n + 1] - flux[0:n])


def with_ghost_lanes(x):
    rows, cells = x.shape
    lane = lax.broadcasted_iota(jnp.int32, (rows, 128), 1)
    last = jnp.broadcast_to(x[:, cells - 1 : cells], (rows, 128))
    first = jnp.broadcast_to(x[:, 0:1], (rows, 128))
    return jnp.concatenate([x, jnp.where(lane < 64, last, first)], axis=1)


def sweep_lanes(q, a0, a1, a2, rate):
    width = q.shape[1]
    cells = width - 128
    before = pltpu.roll(q, 1, 1)
    face = clipped_interface(pltpu.roll(q, 2, 1), before, q, pltpu.roll(q, width - 1, 1))
    right = pltpu.roll(face, width - 1, 1)
    spread = right - face
    curvature = 6.0 * (q - 0.5 * (face + right))
    up = a0 > 0
    flux = (
        a0 * face
        + a1 * jnp.where(up, pltpu.roll(curvature, 1, 1), curvature)
        + a2 * jnp.where(up, pltpu.roll(spread, 1, 1), spread)
    )
    change = pltpu.roll(flux, width - 1, 1) - flux
    return q[:, :cells] - rate * change[:, :cells]


def put(ref, index, rows, value):
    for c in range(value.shape[1] // 128):
        ref[index, c, rows, :] = value[:, 128 * c : 128 * c + 128]


def get(ref, index, rows):
    return jnp.concatenate([ref[index, c, rows, :] for c in range(ref.shape[1])], axis=1)


def kernel(
    sizes,
    state_hbm,
    velocity_hbm,
    donor_hbm,
    weight_hbm,
    out_ref,
    own,
    vel,
    donor_ref,
    weight_ref,
    rad_ext,
    rad_vel,
    stage,
    ang_ext,
    ang_vel,
    azi_coef,
    swept,
    planes,
    split,
    onehot,
    near_weight,
    far_weight,
    zone_sum,
    theta_out,
    phi_out,
    theta_in,
    phi_in,
    phi_rows,
    local_sem,
    halo_send,
    halo_recv,
    plane_send,
    plane_recv,
    zone_send,
    theta_recv,
    phi_recv,
    token_sem,
):
    n_rad, n_ang, groups, nr, nt, nphi, theta_cells, zones = sizes
    panel = lax.axis_index("panel")
    rad = lax.axis_index("rad")
    ang = lax.axis_index("ang")
    twin = 1 - panel
    theta_step, phi_step, radius_step, theta_start, time_step = geometry(theta_cells, nphi)
    first_owner = 2
    owners = groups * nr
    is_owner = (ang >= first_owner) & (ang < first_owner + owners)

    load_state = pltpu.make_async_copy(state_hbm, own, local_sem.at[0])
    load_velocity = pltpu.make_async_copy(velocity_hbm, vel, local_sem.at[1])
    load_donor = pltpu.make_async_copy(donor_hbm, donor_ref, local_sem.at[2])
    load_weight = pltpu.make_async_copy(weight_hbm, weight_ref, local_sem.at[3])
    for load in (load_state, load_velocity, load_donor, load_weight):
        load.start()

    rad_down, rad_up = (panel, rad - 1, ang), (panel, rad + 1, ang)
    ang_down, ang_up = (panel, rad, ang - 1), (panel, rad, ang + 1)
    has_rad = (rad > 0, rad < n_rad - 1)
    has_ang = (ang > 0, ang < n_ang - 1)

    barrier = pltpu.get_barrier_semaphore()
    for exists, device in zip(has_rad, (rad_down, rad_up)):

        @pl.when(exists)
        def _():
            pl.semaphore_signal(barrier, inc=1, device_id=device, device_id_type=MESH)

    def ring(distance):
        return (panel, rad, lax.rem(ang + distance + n_ang, n_ang))

    for device in (ring(-1), ring(1), (twin, rad, ang)):
        pl.semaphore_signal(barrier, inc=1, device_id=device, device_id_type=MESH)

    load_state.wait()
    load_velocity.wait()
    for g in range(groups):
        for f in range(2):
            for r in range(nr):
                rad_ext[g, 3 + r, f * nt : (f + 1) * nt, :] = own[2 * g + f, r]
    for r in range(nr):
        for f in range(2):
            rad_vel[1 + r, f * nt : (f + 1) * nt, :] = vel[0, r]
            row = (2 * r + f) * nt
            put(stage, groups, pl.ds(row, nt), vel[1, r])
            put(stage, groups + 1, pl.ds(row, nt), vel[2, r])
    for t in range(nt):
        ang_vel[1 + t] = get(stage, groups, pl.ds(t, 2 * nr, stride=nt))

    def edges(has, fills):
        for exists, fill in zip(has, fills):
            pl.when(jnp.logical_not(exists))(fill)

    def fill_rad(source, ends, buffers):
        def fill():
            rad_vel[ends[1]] = rad_vel[source]
            for g in range(groups):
                for i in buffers:
                    rad_ext[g, i] = rad_ext[g, source + 2]

        return fill

    def fill_ang_vel(source, end):
        def fill():
            ang_vel[end] = ang_vel[source]

        return fill

    edges(
        has_rad,
        (
            fill_rad(1, (1, 0), range(3)),
            fill_rad(nr, (nr, nr + 1), range(nr + 3, nr + 6)),
        ),
    )
    edges(has_ang, (fill_ang_vel(1, 0), fill_ang_vel(nt, nt + 1)))

    pl.semaphore_wait(
        barrier, 3 + jnp.where(rad > 0, 1, 0) + jnp.where(rad < n_rad - 1, 1, 0)
    )

    def send(src, dst, slot, device):
        return pltpu.make_async_remote_copy(
            src_ref=src,
            dst_ref=dst,
            send_sem=halo_send.at[slot],
            recv_sem=halo_recv.at[slot],
            device_id=device,
            device_id_type=MESH,
        )

    def both(has, pair, act):
        down, up = pair

        @pl.when(has[0])
        def _():
            act(down, up)

        @pl.when(has[1])
        def _():
            act(up, down)

    def start(mine, theirs):
        mine().start()

    def wait_send(mine, theirs):
        mine().wait_send()

    def wait_recv(mine, theirs):
        theirs().wait_recv()

    def rad_copies(g):
        return (
            lambda: send(rad_ext.at[g, 3:6], rad_ext.at[g, nr + 3 : nr + 6], 4 * g, rad_down),
            lambda: send(rad_ext.at[g, nr : nr + 3], rad_ext.at[g, 0:3], 4 * g + 1, rad_up),
        )

    def ang_copies(g):
        return (
            lambda: send(ang_ext.at[g, 3:6], ang_ext.at[g, nt + 3 : nt + 6], 4 * g + 2, ang_down),
            lambda: send(ang_ext.at[g, nt : nt + 3], ang_ext.at[g, 0:3], 4 * g + 3, ang_up),
        )

    base = 4 * groups
    rad_vel_copies = (
        lambda: send(rad_vel.at[1], rad_vel.at[nr + 1], base, rad_down),
        lambda: send(rad_vel.at[nr], rad_vel.at[0], base + 1, rad_up),
    )
    ang_vel_copies = (
        lambda: send(ang_vel.at[1], ang_vel.at[nt + 1], base + 2, ang_down),
        lambda: send(ang_vel.at[nt], ang_vel.at[0], base + 3, ang_up),
    )
    both(has_rad, rad_vel_copies, start)
    for g in range(groups):
        both(has_rad, rad_copies(g), start)
    both(has_ang, ang_vel_copies, start)

    def tell(level):
        for distance in (-(2**level), 2**level):
            pl.semaphore_signal(
                token_sem.at[level], inc=1, device_id=ring(distance), device_id_type=MESH
            )

    def hear(level):
        pl.semaphore_wait(token_sem.at[level], 2)

    tell(0)
    load_donor.wait()
    load_weight.wait()

    @pl.when(is_owner)
    def _():
        donor_all = donor_ref[...]
        donor = jnp.where(panel == 0, donor_all[1:2], donor_all[0:1]).astype(F32)
        donor_row = jnp.floor((donor + 0.5) * (1.0 / nphi))
        donor_col = donor - donor_row * nphi
        weights = jnp.where(panel == 0, weight_ref[1], weight_ref[0])
        cells = 2 * theta_cells
        row_of = lax.broadcasted_iota(jnp.int32, (cells, 128), 0)
        row_of = ((row_of // (2 * nt)) * nt + lax.rem(row_of, nt)).astype(F32)
        col_of = lax.broadcasted_iota(jnp.int32, (nphi, 128), 0).astype(F32)
        for z in range(0, zones, 128):
            here = donor_row[:, z : z + 128]
            w = weights[:, z : z + 128]
            at_row = row_of == here
            above = row_of == here + 1.0
            near_weight[:, z : z + 128] = jnp.where(
                at_row, w[0:1], jnp.where(above, w[2:3], 0.0)
            )
            far_weight[:, z : z + 128] = jnp.where(
                at_row, w[1:2], jnp.where(above, w[3:4], 0.0)
            )
            hot = jnp.where(col_of == donor_col[:, z : z + 128], 1.0, 0.0).astype(BF16)
            onehot[0:nphi, z : z + 128] = hot
            onehot[nphi : 2 * nphi, z : z + 128] = hot

    hear(0)
    tell(1)

    def wide(x, tiles):
        return jnp.concatenate([x] * tiles, axis=-1)

    tiles = nphi // 128
    lead = lambda n: lax.broadcasted_iota(jnp.int32, (n, 8, 128), 0)
    sub = lambda n: lax.broadcasted_iota(jnp.int32, (n, 8, 128), 1)
    radius_of_row = (
        INNER_RADIUS + ((rad * nr + sub(nt) // 2).astype(F32) + 0.5) * radius_step
    )
    theta_cell = theta_start + ((ang * nt + lead(nt)).astype(F32) + 0.5) * theta_step
    sin_cell = jnp.sin(theta_cell)
    polar_rate = wide(time_step / (radius_of_row * sin_cell * theta_step), tiles)
    azimuth_rate = time_step / (radius_of_row * sin_cell * phi_step)
    azimuth_rate = azimuth_rate.reshape(nt * 8, 128)
    azi_u = jnp.concatenate(
        [get(stage, groups + 1, pl.ds(t, 2 * nr, stride=nt)) for t in range(nt)], axis=0
    )
    azi_u = with_ghost_lanes(azi_u)
    azi_face = 0.5 * (azi_u + pltpu.roll(azi_u, 1, 1))
    for i, coefficient in enumerate(
        flux_coefficients(azi_face, None, wide(azimuth_rate, tiles + 1))
    ):
        azi_coef[i] = coefficient
    azimuth_rate = wide(azimuth_rate, tiles)

    hear(1)
    tell(2)

    both(has_rad, rad_vel_copies, wait_recv)
    v = rad_vel[...]
    radius_face = INNER_RADIUS + (rad * nr + lead(nr + 1)).astype(F32) * radius_step
    radius_cell = INNER_RADIUS + ((rad * nr + lead(nr)).astype(F32) + 0.5) * radius_step
    rad_coef = flux_coefficients(
        0.5 * (v[0 : nr + 1] + v[1 : nr + 2]),
        wide(radius_face * radius_face, tiles),
        time_step / radius_step,
    )
    rad_rate = wide(time_step / (radius_cell * radius_cell * radius_step), tiles)
    for g in range(groups):
        both(has_rad, rad_copies(g), wait_recv)
        after = sweep_leading(rad_ext[g], *rad_coef, rad_rate)
        for r in range(nr):
            put(stage, g, pl.ds(8 * r, 8), after[r])
        for t in range(nt):
            ang_ext[g, 3 + t] = get(stage, g, pl.ds(t, 2 * nr, stride=nt))
        both(has_ang, ang_copies(g), start)

        def fill_ang(source, targets):
            def fill():
                for i in targets:
                    ang_ext[g, i] = ang_ext[g, source]

            return fill

        edges(
            has_ang,
            (fill_ang(3, range(3)), fill_ang(nt + 2, range(nt + 3, nt + 6))),
        )

    both(has_ang, ang_vel_copies, wait_recv)
    v = ang_vel[...]
    theta_face = theta_start + (ang * nt + lead(nt + 1)).astype(F32) * theta_step
    radius_of_face = INNER_RADIUS + ((rad * nr + sub(nt + 1) // 2).astype(F32) + 0.5) * radius_step
    ang_coef = flux_coefficients(
        0.5 * (v[0 : nt + 1] + v[1 : nt + 2]),
        wide(jnp.sin(theta_face), tiles),
        wide(time_step / (radius_of_face * theta_step), tiles),
    )

    def plane_copy(g, r):
        return pltpu.make_async_remote_copy(
            src_ref=swept.at[g, :, 8 * r : 8 * r + 8],
            dst_ref=planes.at[ang],
            send_sem=plane_send.at[g * nr + r],
            recv_sem=plane_recv,
            device_id=(panel, rad, first_owner + g * nr + r),
            device_id_type=MESH,
        )

    hear(2)
    for g in range(groups):
        both(has_ang, ang_copies(g), wait_recv)
        polar = sweep_leading(ang_ext[g], *ang_coef, polar_rate)
        cells = with_ghost_lanes(polar.reshape(nt * 8, nphi))
        done = sweep_lanes(cells, azi_coef[0], azi_coef[1], azi_coef[2], azimuth_rate)
        for t in range(nt):
            put(swept, g, pl.ds(t, 2 * nr, stride=nt), done[8 * t : 8 * t + 8])
        for r in range(nr):
            @pl.when(ang != first_owner + g * nr + r)
            def _():
                plane_copy(g, r).start()

            @pl.when(ang == first_owner + g * nr + r)
            def _():
                pltpu.make_async_copy(
                    swept.at[g, :, 8 * r : 8 * r + 8], planes.at[ang], plane_recv
                ).start()

    def zone_copies():
        order = ang - first_owner
        copies = []
        for side, target in ((0, 0), (1, n_ang - 1)):
            copies.append(
                pltpu.make_async_remote_copy(
                    src_ref=theta_out.at[side],
                    dst_ref=theta_in.at[order],
                    send_sem=zone_send.at[n_ang + side],
                    recv_sem=theta_recv,
                    device_id=(twin, rad, target),
                    device_id_type=MESH,
                )
            )
        for target in range(n_ang):
            copies.append(
                pltpu.make_async_remote_copy(
                    src_ref=phi_out.at[target // (n_ang // 2)],
                    dst_ref=phi_in.at[order],
                    send_sem=zone_send.at[target],
                    recv_sem=phi_recv,
                    device_id=(twin, rad, target),
                    device_id_type=MESH,
                )
            )
        return copies

    @pl.when(is_owner)
    def _():
        pltpu.make_async_copy(planes, planes, plane_recv).wait()
        cells = 2 * theta_cells
        x = jnp.concatenate(
            [planes[:, c].reshape(cells, 128) for c in range(nphi // 128)], axis=1
        )
        for i, part in enumerate((x, pltpu.roll(x, nphi - 1, 1))):
            high = part.astype(BF16)
            split[i * cells : (i + 1) * cells, 0:nphi] = high
            split[i * cells : (i + 1) * cells, nphi : 2 * nphi] = (
                part - high.astype(F32)
            ).astype(BF16)
        x = split[...]
        for z in range(0, zones, 256):
            y = jnp.dot(x, onehot[:, z : z + 256], preferred_element_type=F32)
            picked = (
                near_weight[:, z : z + 256] * y[:cells] + far_weight[:, z : z + 256] * y[cells:]
            )
            zone_sum[:, z : z + 256] = picked.reshape(n_ang, 2 * nt, 256).sum(axis=0)
        for f in range(2):
            line = jnp.sum(zone_sum[f * nt : (f + 1) * nt, :], axis=0, keepdims=True)
            for side in range(2):
                for row in range(G):
                    start = (side * G + row) * nphi
                    theta_out[side, row, f : f + 1, :] = line[:, start : start + nphi]
                start = 2 * G * nphi + side * 128
                phi_out[side, f : f + 1, :] = line[:, start : start + 128]
        for copy in zone_copies():
            copy.start()

    pltpu.make_async_copy(phi_in, phi_in, phi_recv).wait()
    for g in range(groups):
        for r in range(nr):
            @pl.when(ang != first_owner + g * nr + r)
            def _():
                plane_copy(g, r).wait_send()

    for o in range(owners):
        phi_rows[2 * o : 2 * o + 2, :] = phi_in[o]
    rows = phi_rows[...]
    lane = lax.broadcasted_iota(jnp.int32, (8, 128), 1)
    start = lax.rem(ang, n_ang // 2) * (2 * G * nt)
    for t in range(nt):
        left = pltpu.roll(rows, lax.rem(256 - start - 2 * G * t, 128), 1)
        right = pltpu.roll(rows, lax.rem(256 - start - 2 * G * t - 2 * G, 128), 1)
        for g in range(groups):
            line = get(swept, g, pl.ds(t, 2 * nr, stride=nt))
            line = jnp.concatenate(
                [
                    jnp.where(lane < G, left[8 * g : 8 * g + 8], line[:, :128]),
                    line[:, 128 : nphi - 128],
                    jnp.where(lane >= 128 - G, right[8 * g : 8 * g + 8], line[:, nphi - 128 :]),
                ],
                axis=1,
            )
            put(stage, g, pl.ds(t, 2 * nr, stride=nt), line)

    def fill_rows(first_row):
        pltpu.make_async_copy(theta_in, theta_in, theta_recv).wait()
        for row in range(G):
            for g in range(groups):
                for r in range(nr):
                    ang_ext[g, row, 2 * r : 2 * r + 2, :] = theta_in[g * nr + r, row]
                put(stage, g, pl.ds(first_row + row, 2 * nr, stride=nt), ang_ext[g, row])

    @pl.when(ang == 0)
    def _():
        fill_rows(0)

    @pl.when(ang == n_ang - 1)
    def _():
        fill_rows(nt - G)

    for g in range(groups):
        for f in range(2):
            for r in range(nr):
                row = (2 * r + f) * nt
                out_ref[2 * g + f, r] = get(stage, g, pl.ds(row, nt))

    both(has_rad, rad_vel_copies, wait_send)
    both(has_ang, ang_vel_copies, wait_send)
    for g in range(groups):
        both(has_rad, rad_copies(g), wait_send)
        both(has_ang, ang_copies(g), wait_send)

    @pl.when(is_owner)
    def _():
        for copy in zone_copies():
            copy.wait_send()


def solution(mesh):
    n_rad, n_ang = mesh.shape["rad"], mesh.shape["ang"]

    def body(state, velocity, band_donor, band_weight):
        _, fields, nr, nt, nphi = state.shape
        zones = band_donor.shape[1]
        groups = fields // 2
        owners = groups * nr
        theta_cells = nt * n_ang
        sizes = (n_rad, n_ang, groups, nr, nt, nphi, theta_cells, zones)
        n_halo = 4 * groups + 4
        out = pl.pallas_call(
            functools.partial(kernel, sizes),
            out_shape=jax.ShapeDtypeStruct((fields, nr, nt, nphi), F32),
            in_specs=[pl.BlockSpec(memory_space=pltpu.HBM)] * 4,
            out_specs=pl.BlockSpec(memory_space=pltpu.VMEM),
            scratch_shapes=[
                pltpu.VMEM((fields, nr, nt, nphi), F32),
                pltpu.VMEM((3, nr, nt, nphi), F32),
                pltpu.VMEM((2, zones), jnp.int32),
                pltpu.VMEM((2, 4, zones), F32),
                pltpu.VMEM((groups, nr + 6, 8, nphi), F32),
                pltpu.VMEM((nr + 2, 8, nphi), F32),
                pltpu.VMEM((groups + 2, nphi // 128, 8 * nr, 128), F32),
                pltpu.VMEM((groups, nt + 6, 8, nphi), F32),
                pltpu.VMEM((nt + 2, 8, nphi), F32),
                pltpu.VMEM((3, 8 * nt, nphi + 128), F32),
                pltpu.VMEM((groups, nphi // 128, 8 * nr, 128), F32),
                pltpu.VMEM((n_ang, nphi // 128, 2 * nt, 128), F32),
                pltpu.VMEM((4 * theta_cells, 2 * nphi), BF16),
                pltpu.VMEM((2 * nphi, zones), BF16),
                pltpu.VMEM((2 * theta_cells, zones), F32),
                pltpu.VMEM((2 * theta_cells, zones), F32),
                pltpu.VMEM((2 * nt, zones), F32),
                pltpu.VMEM((2, G, 2, nphi), F32),
                pltpu.VMEM((2, 2, 128), F32),
                pltpu.VMEM((owners, G, 2, nphi), F32),
                pltpu.VMEM((owners, 2, 128), F32),
                pltpu.VMEM((2 * owners, 128), F32),
                pltpu.SemaphoreType.DMA((4,)),
                pltpu.SemaphoreType.DMA((n_halo,)),
                pltpu.SemaphoreType.DMA((n_halo,)),
                pltpu.SemaphoreType.DMA((owners,)),
                pltpu.SemaphoreType.DMA,
                pltpu.SemaphoreType.DMA((n_ang + 2,)),
                pltpu.SemaphoreType.DMA,
                pltpu.SemaphoreType.DMA,
                pltpu.SemaphoreType.REGULAR((3,)),
            ],
            compiler_params=pltpu.CompilerParams(
                collective_id=0, has_side_effects=True, vmem_limit_bytes=64 * 1024 * 1024
            ),
        )(state[0], velocity[0], band_donor, band_weight)
        return out[None]

    spec = P("panel", None, "rad", "ang", None)
    return jax.shard_map(
        body, mesh=mesh, in_specs=(spec, spec, P(), P()), out_specs=spec, check_vma=False
    )
```

```python
import functools
import math

import jax
import jax.numpy as jnp
from jax import lax
from jax.experimental import pallas as pl
from jax.experimental.pallas import tpu as pltpu
from jax.sharding import PartitionSpec as P

G = 2
INNER_RADIUS = 1.0
COURANT = 0.8
MESH = pl.DeviceIdType.MESH
F32 = jnp.float32
BF16 = jnp.bfloat16


def geometry(theta_cells, phi_cells):
    theta_step = math.pi / 2 / (theta_cells - 2 * G)
    phi_step = 1.5 * math.pi / (phi_cells - 2 * G)
    radius_step = INNER_RADIUS * theta_step
    theta_start = math.pi / 4 - G * theta_step
    time_step = COURANT * INNER_RADIUS * min(theta_step, math.sin(theta_start) * phi_step)
    return theta_step, phi_step, radius_step, theta_start, time_step


def flux_coefficients(face_speed, area, face_rate):
    size = jnp.abs(face_speed)
    courant = size * face_rate
    half = 0.5 * courant
    a0 = face_speed if area is None else area * face_speed
    a1 = a0 * (half * (1.0 - 2.0 / 3.0 * courant))
    a2 = -(half * (size if area is None else area * size))
    return a0, a1, a2


def clipped_interface(before, left, right, after):
    value = 7.0 / 12.0 * (left + right) - 1.0 / 12.0 * (before + after)
    return jnp.minimum(jnp.maximum(value, jnp.minimum(left, right)), jnp.maximum(left, right))


def sweep_leading(q, a0, a1, a2, rate):
    n = q.shape[0] - 6
    face = clipped_interface(q[0 : n + 3], q[1 : n + 4], q[2 : n + 5], q[3 : n + 6])
    left, right = face[0 : n + 2], face[1 : n + 3]
    spread = right - left
    curvature = 6.0 * (q[2 : n + 4] - 0.5 * (left + right))
    up = a0 > 0
    flux = (
        a0 * face[1 : n + 2]
        + a1 * jnp.where(up, curvature[0 : n + 1], curvature[1 : n + 2])
        + a2 * jnp.where(up, spread[0 : n + 1], spread[1 : n + 2])
    )
    return q[3 : n + 3] - rate * (flux[1 : n + 1] - flux[0:n])


def with_ghost_lanes(x):
    rows, cells = x.shape
    lane = lax.broadcasted_iota(jnp.int32, (rows, 128), 1)
    last = jnp.broadcast_to(x[:, cells - 1 : cells], (rows, 128))
    first = jnp.broadcast_to(x[:, 0:1], (rows, 128))
    return jnp.concatenate([x, jnp.where(lane < 64, last, first)], axis=1)


def sweep_rolled(q, a0, a1, a2, axis):
    width = q.shape[axis]

    def ahead(x):
        return pltpu.roll(x, width - 1, axis)

    def behind(x):
        return pltpu.roll(x, 1, axis)

    face = clipped_interface(pltpu.roll(q, 2, axis), behind(q), q, ahead(q))
    right = ahead(face)
    spread = right - face
    curvature = 6.0 * (q - 0.5 * (face + right))
    up = a0 > 0
    flux = (
        a0 * face
        + a1 * jnp.where(up, behind(curvature), curvature)
        + a2 * jnp.where(up, behind(spread), spread)
    )
    return ahead(flux) - flux


def put(ref, index, rows, value):
    for c in range(value.shape[1] // 128):
        ref[index, c, rows, :] = value[:, 128 * c : 128 * c + 128]


def kernel(
    sizes,
    state_hbm,
    velocity_hbm,
    donor_hbm,
    weight_hbm,
    out_ref,
    own,
    vel,
    donor_ref,
    weight_ref,
    rad_ext,
    rad_vel,
    halo,
    halo_vel,
    stage,
    planes,
    planes_vel,
    block_vel,
    polar_coef,
    azimuth_coef,
    block,
    split,
    onehot,
    near_weight,
    far_weight,
    zone_sum,
    zone_out,
    theta_in,
    phi_in,
    back_out,
    result,
    local_sem,
    halo_send,
    halo_recv,
    plane_send,
    plane_recv,
    zone_send,
    theta_recv,
    phi_recv,
    back_send,
    back_recv,
    token_sem,
):
    n_rad, n_ang, groups, nr, nt, nphi, theta_cells, zones = sizes
    panel = lax.axis_index("panel")
    rad = lax.axis_index("rad")
    ang = lax.axis_index("ang")
    twin = 1 - panel
    theta_step, phi_step, radius_step, theta_start, time_step = geometry(theta_cells, nphi)
    row_index, member = ang // nr, lax.rem(ang, nr)
    row_cells = nr * nt
    fields = 2 * groups
    tiles = nphi // 128
    theta_tiles = 2 * G * tiles

    load_state = pltpu.make_async_copy(state_hbm, own, local_sem.at[0])
    load_velocity = pltpu.make_async_copy(velocity_hbm, vel, local_sem.at[1])
    load_donor = pltpu.make_async_copy(donor_hbm, donor_ref, local_sem.at[2])
    load_weight = pltpu.make_async_copy(weight_hbm, weight_ref, local_sem.at[3])
    for load in (load_state, load_velocity, load_donor, load_weight):
        load.start()

    rad_down, rad_up = (panel, rad - 1, ang), (panel, rad + 1, ang)
    has_rad = (rad > 0, rad < n_rad - 1)

    barrier = pltpu.get_barrier_semaphore()
    for exists, device in zip(has_rad, (rad_down, rad_up)):

        @pl.when(exists)
        def _():
            pl.semaphore_signal(barrier, inc=1, device_id=device, device_id_type=MESH)

    def ring(distance):
        return (panel, rad, lax.rem(ang + distance + n_ang, n_ang))

    for device in (ring(-1), ring(1), (twin, rad, ang)):
        pl.semaphore_signal(barrier, inc=1, device_id=device, device_id_type=MESH)

    pl.semaphore_wait(
        barrier, 3 + jnp.where(rad > 0, 1, 0) + jnp.where(rad < n_rad - 1, 1, 0)
    )

    def send(src, dst, slot, device):
        return pltpu.make_async_remote_copy(
            src_ref=src,
            dst_ref=dst,
            send_sem=halo_send.at[slot],
            recv_sem=halo_recv.at[slot],
            device_id=device,
            device_id_type=MESH,
        )

    def both(has, pair, act):
        down, up = pair

        @pl.when(has[0])
        def _():
            act(down, up)

        @pl.when(has[1])
        def _():
            act(up, down)

    def start(mine, theirs):
        mine().start()

    def wait_send(mine, theirs):
        mine().wait_send()

    def wait_recv(mine, theirs):
        theirs().wait_recv()

    def rad_copies(g):
        return (
            lambda: send(state_hbm.at[pl.ds(2 * g, 2), pl.ds(0, 3)], halo.at[g, 1], 2 * g, rad_down),
            lambda: send(
                state_hbm.at[pl.ds(2 * g, 2), pl.ds(nr - 3, 3)], halo.at[g, 0], 2 * g + 1, rad_up
            ),
        )

    base = 2 * groups
    rad_vel_copies = (
        lambda: send(velocity_hbm.at[0, 0], halo_vel.at[1], base, rad_down),
        lambda: send(velocity_hbm.at[0, nr - 1], halo_vel.at[0], base + 1, rad_up),
    )
    both(has_rad, rad_vel_copies, start)
    for g in range(groups):
        both(has_rad, rad_copies(g), start)
    def tell(level):
        for distance in (-(2**level), 2**level):
            pl.semaphore_signal(
                token_sem.at[level], inc=1, device_id=ring(distance), device_id_type=MESH
            )

    def hear(level):
        pl.semaphore_wait(token_sem.at[level], 2)

    tell(0)
    load_state.wait()
    load_velocity.wait()
    for g in range(groups):
        for f in range(2):
            for r in range(nr):
                rad_ext[g, 3 + r, f * nt : (f + 1) * nt, :] = own[2 * g + f, r]
    for r in range(nr):
        for f in range(2):
            rad_vel[1 + r, f * nt : (f + 1) * nt, :] = vel[0, r]

    def edges(has, fills):
        for exists, fill in zip(has, fills):
            pl.when(jnp.logical_not(exists))(fill)

    def fill_rad(source, ends, buffers):
        def fill():
            rad_vel[ends[1]] = rad_vel[source]
            for g in range(groups):
                for i in buffers:
                    rad_ext[g, i] = rad_ext[g, source + 2]

        return fill

    edges(
        has_rad,
        (
            fill_rad(1, (1, 0), range(3)),
            fill_rad(nr, (nr, nr + 1), range(nr + 3, nr + 6)),
        ),
    )


    load_donor.wait()
    load_weight.wait()

    donor_all = donor_ref[...]
    donor = jnp.where(panel == 0, donor_all[1:2], donor_all[0:1]).astype(F32)
    donor_row = jnp.floor((donor + 0.5) * (1.0 / nphi))
    donor_col = donor - donor_row * nphi
    weights = jnp.where(panel == 0, weight_ref[1], weight_ref[0])
    row_of = lax.broadcasted_iota(jnp.int32, (row_cells, 128), 0)
    row_of = (row_index * row_cells + row_of).astype(F32)
    col_of = lax.broadcasted_iota(jnp.int32, (nphi, 128), 0).astype(F32)
    for z in range(0, zones, 128):
        here = donor_row[:, z : z + 128]
        w = weights[:, z : z + 128]
        at_row = row_of == here
        above = row_of == here + 1.0
        near_weight[:, z : z + 128] = jnp.where(at_row, w[0:1], jnp.where(above, w[2:3], 0.0))
        far_weight[:, z : z + 128] = jnp.where(at_row, w[1:2], jnp.where(above, w[3:4], 0.0))
        hot = jnp.where(col_of == donor_col[:, z : z + 128], 1.0, 0.0).astype(BF16)
        onehot[0:nphi, z : z + 128] = hot
        onehot[nphi : 2 * nphi, z : z + 128] = hot

    hear(0)
    tell(1)

    def wide(x, tiles):
        return jnp.concatenate([x] * tiles, axis=-1)

    hear(1)
    tell(2)

    has_block = (row_index > 0, row_index < n_ang // nr - 1)

    def exchange(source, target, sends, recvs):
        def to(other_row, k, slot, send_slot, recv_slot):
            return pltpu.make_async_remote_copy(
                src_ref=source(k),
                dst_ref=target.at[slot],
                send_sem=sends.at[send_slot],
                recv_sem=recvs.at[recv_slot],
                device_id=(panel, rad, other_row * nr + k),
                device_id_type=MESH,
            )

        def all_remote(act):
            for step in range(1, nr):
                act(to(row_index, lax.rem(member + step, nr), member + 1, step, 0))

            @pl.when(has_block[1] & (member == nr - 1))
            def _():
                for k in range(nr):
                    act(to(row_index + 1, k, 0, nr + k, 1))

            @pl.when(has_block[0] & (member == 0))
            def _():
                for k in range(nr):
                    act(to(row_index - 1, k, nr + 1, 2 * nr + k, 2))

        def begin():
            all_remote(lambda copy: copy.start())
            pltpu.make_async_copy(source(member), target.at[member + 1], recvs.at[0]).start()

        def arrive():
            members = target.at[pl.ds(1, nr)]
            pltpu.make_async_copy(members, members, recvs.at[0]).wait()
            for side, slot in ((0, 0), (1, nr + 1)):

                @pl.when(has_block[side])
                def _():
                    edge = target.at[slot]
                    pltpu.make_async_copy(edge, edge, recvs.at[1 + side]).wait()

        def finish():
            all_remote(lambda copy: copy.wait_send())

        return begin, arrive, finish

    vel_begin, vel_arrive, vel_finish = exchange(
        lambda k: velocity_hbm.at[pl.ds(1, 2), k], planes_vel, plane_send.at[0], plane_recv.at[0]
    )
    plane_begin, plane_arrive, plane_finish = exchange(
        lambda k: stage.at[:, :, pl.ds(pl.multiple_of(8 * k, 8), 8)],
        planes,
        plane_send.at[1],
        plane_recv.at[1],
    )
    vel_begin()

    def lead(n):
        return lax.broadcasted_iota(jnp.int32, (n, 8, 128), 0)


    both(has_rad, rad_vel_copies, wait_recv)
    for side, end in ((0, 0), (1, nr + 1)):

        @pl.when(has_rad[side])
        def _():
            for f in range(2):
                rad_vel[end, f * nt : (f + 1) * nt, :] = halo_vel[side]

    v = rad_vel[...]
    radius_face = INNER_RADIUS + (rad * nr + lead(nr + 1)).astype(F32) * radius_step
    radius_cell = INNER_RADIUS + ((rad * nr + lead(nr)).astype(F32) + 0.5) * radius_step
    rad_coef = flux_coefficients(
        0.5 * (v[0 : nr + 1] + v[1 : nr + 2]),
        wide(radius_face * radius_face, tiles),
        time_step / radius_step,
    )
    rad_rate = wide(time_step / (radius_cell * radius_cell * radius_step), tiles)
    for g in range(groups):
        both(has_rad, rad_copies(g), wait_recv)
        for side, first in ((0, 0), (1, nr + 3)):

            @pl.when(has_rad[side])
            def _():
                for f in range(2):
                    for i in range(3):
                        rad_ext[g, first + i, f * nt : (f + 1) * nt, :] = halo[g, side, f, i]

        after = sweep_leading(rad_ext[g], *rad_coef, rad_rate)
        for r in range(nr):
            put(stage, g, pl.ds(8 * r, 8), after[r])
    plane_begin()

    vel_arrive()
    for slot in range(nr + 2):
        block_vel[0, slot * nt : (slot + 1) * nt, :] = planes_vel[slot, 0]
    for slot in range(nr):
        block_vel[1, slot * nt : (slot + 1) * nt, :] = planes_vel[slot + 1, 1]
    ext = row_cells + 2 * nt
    ghosts = ((0, nt, nt), (nt + row_cells, ext, nt + row_cells - 1))

    def fill_ghosts(ref, index):
        for side, (first, last, source) in enumerate(ghosts):

            @pl.when(jnp.logical_not(has_block[side]))
            def _():
                for i in index:
                    ref[i, first:last, :] = jnp.broadcast_to(
                        ref[i, source : source + 1, :], (nt, nphi)
                    )

    fill_ghosts(block_vel, range(1))

    def places(n, first):
        return lax.broadcasted_iota(jnp.int32, (n, 128), 0) + (row_index * row_cells + first)

    def shell_radius(n):
        shell = jnp.zeros((n, 128), jnp.int32) + (rad * nr + member)
        return INNER_RADIUS + (shell.astype(F32) + 0.5) * radius_step

    face_place = places(ext, -nt).astype(F32)
    radius = shell_radius(ext)
    u = block_vel[0, 0:ext, :]
    for i, coefficient in enumerate(
        flux_coefficients(
            0.5 * (u + pltpu.roll(u, 1, 0)),
            wide(jnp.sin(theta_start + face_place * theta_step), tiles),
            wide(time_step / (radius * theta_step), tiles),
        )
    ):
        polar_coef[i] = coefficient
    sin_cell = jnp.sin(theta_start + (face_place + 0.5) * theta_step)
    polar_coef[3] = wide(time_step / (radius * sin_cell * theta_step), tiles)
    sin_cell = jnp.sin(theta_start + (places(row_cells, 0).astype(F32) + 0.5) * theta_step)
    rate = wide(time_step / (shell_radius(row_cells) * sin_cell * phi_step), tiles + 1)
    u = with_ghost_lanes(block_vel[1, 0:row_cells, :])
    for i, coefficient in enumerate(
        flux_coefficients(0.5 * (u + pltpu.roll(u, 1, 1)), None, rate)
    ):
        azimuth_coef[i] = coefficient
    azimuth_coef[3] = rate
    hear(2)
    pl.semaphore_signal(
        token_sem.at[3], inc=1, device_id=(twin, rad, ang), device_id_type=MESH
    )

    plane_arrive()
    for slot in range(nr + 2):
        for g in range(groups):
            for c in range(tiles):
                for f in range(2):
                    block[2 * g + f, slot * nt : (slot + 1) * nt, 128 * c : 128 * c + 128] = planes[
                        slot, g, c, f * nt : (f + 1) * nt, :
                    ]
    fill_ghosts(block, range(fields))
    cells = fields * row_cells
    for f in range(fields):
        q = block[f]
        change = sweep_rolled(q, polar_coef[0], polar_coef[1], polar_coef[2], 0)
        q = (q - polar_coef[3] * change)[nt : nt + row_cells]
        wide_q = with_ghost_lanes(q)
        change = sweep_rolled(wide_q, azimuth_coef[0], azimuth_coef[1], azimuth_coef[2], 1)
        q = (wide_q - azimuth_coef[3] * change)[:, :nphi]
        for k in range(nr):
            for c in range(tiles):
                back_out[k, c, f * nt : (f + 1) * nt, :] = q[
                    k * nt : (k + 1) * nt, 128 * c : 128 * c + 128
                ]
        for i, part in enumerate((q, pltpu.roll(q, nphi - 1, 1))):
            coarse = part.astype(BF16)
            row = i * cells + f * row_cells
            split[row : row + row_cells, 0:nphi] = coarse
            split[row : row + row_cells, nphi : 2 * nphi] = (part - coarse.astype(F32)).astype(BF16)

    def back_copy(step):
        other = lax.rem(member + step, nr)
        return pltpu.make_async_remote_copy(
            src_ref=back_out.at[other],
            dst_ref=result.at[member],
            send_sem=back_send.at[step],
            recv_sem=back_recv,
            device_id=(panel, rad, row_index * nr + other),
            device_id_type=MESH,
        )

    theta_tiles = 2 * G * tiles

    def zone_copies():
        copies = []
        for side, target in ((0, 0), (1, n_ang - 1)):
            copies.append(
                pltpu.make_async_remote_copy(
                    src_ref=zone_out.at[pl.ds(side * theta_tiles // 2, theta_tiles // 2)],
                    dst_ref=theta_in.at[ang],
                    send_sem=zone_send.at[n_ang + side],
                    recv_sem=theta_recv,
                    device_id=(twin, rad, target),
                    device_id_type=MESH,
                )
            )
        for target in range(n_ang):
            copies.append(
                pltpu.make_async_remote_copy(
                    src_ref=zone_out.at[theta_tiles + target // (n_ang // 2)],
                    dst_ref=phi_in.at[ang],
                    send_sem=zone_send.at[target],
                    recv_sem=phi_recv,
                    device_id=(twin, rad, target),
                    device_id_type=MESH,
                )
            )
        return copies

    x = split[...]
    for z in range(0, zones, 256):
        y = jnp.dot(x, onehot[:, z : z + 256], preferred_element_type=F32)
        near = near_weight[:, z : z + 256].reshape(1, row_cells, 256)
        far = far_weight[:, z : z + 256].reshape(1, row_cells, 256)
        picked = near * y[:cells].reshape(fields, row_cells, 256) + far * y[cells:].reshape(
            fields, row_cells, 256
        )
        picked = picked.reshape(fields, row_cells // 8, 8, 256).sum(axis=1).reshape(8 * fields, 256)
        for half in range(2):
            zone_sum[z // 128 + half] = picked[:, 128 * half : 128 * half + 128]
    for z in range(zones // 128):
        parts = [zone_sum[z, pl.ds(t, fields, stride=8), :] for t in range(8)]
        while len(parts) > 1:
            parts = [a + b for a, b in zip(parts[::2], parts[1::2])]
        zone_out[z, 0:fields, :] = parts[0]
    pl.semaphore_wait(token_sem.at[3], 1)
    for copy in zone_copies():
        copy.start()

    for step in range(1, nr):
        back_copy(step).start()
    pltpu.make_async_copy(back_out.at[member], result.at[member], back_recv).start()

    pltpu.make_async_copy(result, result, back_recv).wait()
    pltpu.make_async_copy(phi_in, phi_in, phi_recv).wait()
    lane = lax.broadcasted_iota(jnp.int32, (fields, 128), 1)
    first_lane = lax.rem(ang, n_ang // 2) * (2 * G * nt)
    for r in range(nr):
        total = phi_in[r, 0:fields, :]
        for k in range(1, n_ang // nr):
            total = total + phi_in[k * nr + r, 0:fields, :]
        for t in range(nt):
            shift = 256 - first_lane - 2 * G * t
            left = pltpu.roll(total, lax.rem(shift, 128), 1)
            right = pltpu.roll(total, lax.rem(shift - 2 * G, 128), 1)
            rows = pl.ds(t, fields, stride=nt)
            result[r, 0, rows, :] = jnp.where(lane < G, left, result[r, 0, rows, :])
            result[r, tiles - 1, rows, :] = jnp.where(
                lane >= 128 - G, right, result[r, tiles - 1, rows, :]
            )

    def fill_rows(first_row):
        pltpu.make_async_copy(theta_in, theta_in, theta_recv).wait()
        for r in range(nr):
            total = theta_in[r, :, 0:fields, :]
            for k in range(1, n_ang // nr):
                total = total + theta_in[k * nr + r, :, 0:fields, :]
            for row in range(G):
                for c in range(tiles):
                    result[r, c, pl.ds(first_row + row, fields, stride=nt), :] = total[
                        row * tiles + c
                    ]

    @pl.when(ang == 0)
    def _():
        fill_rows(0)

    @pl.when(ang == n_ang - 1)
    def _():
        fill_rows(nt - G)

    for f in range(fields):
        for r in range(nr):
            out_ref[f, r] = jnp.concatenate(
                [result[r, c, f * nt : (f + 1) * nt, :] for c in range(tiles)], axis=1
            )

    both(has_rad, rad_vel_copies, wait_send)
    for g in range(groups):
        both(has_rad, rad_copies(g), wait_send)
    vel_finish()
    plane_finish()
    for step in range(1, nr):
        back_copy(step).wait_send()
    for copy in zone_copies():
        copy.wait_send()


def solution(mesh):
    n_rad, n_ang = mesh.shape["rad"], mesh.shape["ang"]

    def body(state, velocity, band_donor, band_weight):
        _, fields, nr, nt, nphi = state.shape
        zones = band_donor.shape[1]
        groups = fields // 2
        theta_cells = nt * n_ang
        sizes = (n_rad, n_ang, groups, nr, nt, nphi, theta_cells, zones)
        n_halo = 2 * groups + 2
        tiles, row_cells = nphi // 128, nr * nt
        ext = row_cells + 2 * nt
        out = pl.pallas_call(
            functools.partial(kernel, sizes),
            out_shape=jax.ShapeDtypeStruct((fields, nr, nt, nphi), F32),
            in_specs=[pl.BlockSpec(memory_space=pltpu.HBM)] * 4,
            out_specs=pl.BlockSpec(memory_space=pltpu.VMEM),
            scratch_shapes=[
                pltpu.VMEM((fields, nr, nt, nphi), F32),
                pltpu.VMEM((3, nr, nt, nphi), F32),
                pltpu.VMEM((2, zones), jnp.int32),
                pltpu.VMEM((2, 4, zones), F32),
                pltpu.VMEM((groups, nr + 6, 8, nphi), F32),
                pltpu.VMEM((nr + 2, 8, nphi), F32),
                pltpu.VMEM((groups, 2, 2, 3, nt, nphi), F32),
                pltpu.VMEM((2, nt, nphi), F32),
                pltpu.VMEM((groups, tiles, 8 * nr, 128), F32),
                pltpu.VMEM((nr + 2, groups, tiles, 8, 128), F32),
                pltpu.VMEM((nr + 2, 2, nt, nphi), F32),
                pltpu.VMEM((2, ext, nphi), F32),
                pltpu.VMEM((4, ext, nphi), F32),
                pltpu.VMEM((4, row_cells, nphi + 128), F32),
                pltpu.VMEM((fields, ext, nphi), F32),
                pltpu.VMEM((2 * fields * row_cells, 2 * nphi), BF16),
                pltpu.VMEM((2 * nphi, zones), BF16),
                pltpu.VMEM((row_cells, zones), F32),
                pltpu.VMEM((row_cells, zones), F32),
                pltpu.VMEM((zones // 128, 8 * fields, 128), F32),
                pltpu.VMEM((zones // 128, 8, 128), F32),
                pltpu.VMEM((n_ang, G * tiles, 8, 128), F32),
                pltpu.VMEM((n_ang, 8, 128), F32),
                pltpu.VMEM((nr, tiles, fields * nt, 128), F32),
                pltpu.VMEM((nr, tiles, fields * nt, 128), F32),
                pltpu.SemaphoreType.DMA((4,)),
                pltpu.SemaphoreType.DMA((n_halo,)),
                pltpu.SemaphoreType.DMA((n_halo,)),
                pltpu.SemaphoreType.DMA((2, 3 * nr)),
                pltpu.SemaphoreType.DMA((2, 3)),
                pltpu.SemaphoreType.DMA((n_ang + 2,)),
                pltpu.SemaphoreType.DMA,
                pltpu.SemaphoreType.DMA,
                pltpu.SemaphoreType.DMA((nr,)),
                pltpu.SemaphoreType.DMA,
                pltpu.SemaphoreType.REGULAR((4,)),
            ],
            compiler_params=pltpu.CompilerParams(
                collective_id=0, has_side_effects=True, vmem_limit_bytes=40 * 1024 * 1024
            ),
        )(
            *(
                pltpu.with_memory_space_constraint(x, pltpu.HBM)
                for x in (state[0], velocity[0], band_donor, band_weight)
            )
        )
        return out[None]

    spec = P("panel", None, "rad", "ang", None)
    return jax.shard_map(
        body, mesh=mesh, in_specs=(spec, spec, P(), P()), out_specs=spec, check_vma=False
    )
```

```python
import functools
import math

import jax
import jax.numpy as jnp
from jax import lax
from jax.experimental import pallas as pl
from jax.experimental.pallas import tpu as pltpu
from jax.sharding import PartitionSpec as P

G = 2
INNER_RADIUS = 1.0
COURANT = 0.8
MESH = pl.DeviceIdType.MESH
F32 = jnp.float32
BF16 = jnp.bfloat16


def geometry(theta_cells, phi_cells):
    theta_step = math.pi / 2 / (theta_cells - 2 * G)
    phi_step = 1.5 * math.pi / (phi_cells - 2 * G)
    radius_step = INNER_RADIUS * theta_step
    theta_start = math.pi / 4 - G * theta_step
    time_step = COURANT * INNER_RADIUS * min(theta_step, math.sin(theta_start) * phi_step)
    return theta_step, phi_step, radius_step, theta_start, time_step


def flux_coefficients(face_speed, area, face_rate):
    size = jnp.abs(face_speed)
    courant = size * face_rate
    half = 0.5 * courant
    a0 = face_speed if area is None else area * face_speed
    a1 = a0 * (half * (1.0 - 2.0 / 3.0 * courant))
    a2 = -(half * (size if area is None else area * size))
    return a0, a1, a2


def clipped_interface(before, left, right, after):
    value = 7.0 / 12.0 * (left + right) - 1.0 / 12.0 * (before + after)
    return jnp.minimum(jnp.maximum(value, jnp.minimum(left, right)), jnp.maximum(left, right))


def sweep_leading(q, a0, a1, a2, rate):
    n = q.shape[0] - 6
    face = clipped_interface(q[0 : n + 3], q[1 : n + 4], q[2 : n + 5], q[3 : n + 6])
    left, right = face[0 : n + 2], face[1 : n + 3]
    spread = right - left
    curvature = 6.0 * (q[2 : n + 4] - 0.5 * (left + right))
    up = a0 > 0
    flux = (
        a0 * face[1 : n + 2]
        + a1 * jnp.where(up, curvature[0 : n + 1], curvature[1 : n + 2])
        + a2 * jnp.where(up, spread[0 : n + 1], spread[1 : n + 2])
    )
    return q[3 : n + 3] - rate * (flux[1 : n + 1] - flux[0:n])


def with_ghost_lanes(x):
    rows, cells = x.shape
    lane = lax.broadcasted_iota(jnp.int32, (rows, 128), 1)
    last = jnp.broadcast_to(x[:, cells - 1 : cells], (rows, 128))
    first = jnp.broadcast_to(x[:, 0:1], (rows, 128))
    return jnp.concatenate([x, jnp.where(lane < 64, last, first)], axis=1)


def sweep_rolled(q, a0, a1, a2, axis):
    width = q.shape[axis]

    def ahead(x):
        return pltpu.roll(x, width - 1, axis)

    def behind(x):
        return pltpu.roll(x, 1, axis)

    face = clipped_interface(pltpu.roll(q, 2, axis), behind(q), q, ahead(q))
    right = ahead(face)
    spread = right - face
    curvature = 6.0 * (q - 0.5 * (face + right))
    up = a0 > 0
    flux = (
        a0 * face
        + a1 * jnp.where(up, behind(curvature), curvature)
        + a2 * jnp.where(up, behind(spread), spread)
    )
    return ahead(flux) - flux


def put(ref, index, rows, value):
    for c in range(value.shape[1] // 128):
        ref[index, c, rows, :] = value[:, 128 * c : 128 * c + 128]


def kernel(
    sizes,
    state_hbm,
    velocity_hbm,
    donor_hbm,
    weight_hbm,
    out_ref,
    own,
    vel,
    donor_ref,
    weight_ref,
    rad_ext,
    rad_vel,
    halo,
    halo_vel,
    stage,
    planes,
    planes_vel,
    block_vel,
    polar_coef,
    azimuth_coef,
    block,
    split,
    onehot,
    near_weight,
    far_weight,
    zone_sum,
    zone_out,
    theta_in,
    phi_in,
    back_out,
    result,
    local_sem,
    halo_send,
    halo_recv,
    plane_send,
    plane_recv,
    zone_send,
    theta_recv,
    phi_recv,
    back_send,
    back_recv,
    token_sem,
):
    n_rad, n_ang, groups, nr, nt, nphi, theta_cells, zones = sizes
    panel = lax.axis_index("panel")
    rad = lax.axis_index("rad")
    ang = lax.axis_index("ang")
    twin = 1 - panel
    theta_step, phi_step, radius_step, theta_start, time_step = geometry(theta_cells, nphi)
    row_index, member = ang // nr, lax.rem(ang, nr)
    row_cells = nr * nt
    fields = 2 * groups
    tiles = nphi // 128
    theta_tiles = 2 * G * tiles

    load_state = pltpu.make_async_copy(state_hbm, own, local_sem.at[0])
    load_velocity = pltpu.make_async_copy(velocity_hbm, vel, local_sem.at[1])
    load_donor = pltpu.make_async_copy(donor_hbm, donor_ref, local_sem.at[2])
    load_weight = pltpu.make_async_copy(weight_hbm, weight_ref, local_sem.at[3])
    for load in (load_state, load_velocity, load_donor, load_weight):
        load.start()

    rad_down, rad_up = (panel, rad - 1, ang), (panel, rad + 1, ang)
    has_rad = (rad > 0, rad < n_rad - 1)

    reach = nr
    barrier = pltpu.get_barrier_semaphore()

    def ring(distance, on_panel):
        return (on_panel, rad, lax.rem(ang + distance + n_ang, n_ang))

    def signal(semaphore, device):
        pl.semaphore_signal(semaphore, inc=1, device_id=device, device_id_type=MESH)

    for exists, other in zip(has_rad, (rad - 1, rad + 1)):

        @pl.when(exists)
        def _():
            signal(barrier, (0, other, ang))

    signal(barrier, (twin, rad, ang))
    for distance in range(1, reach + 1):
        signal(barrier, ring(distance, 1))
        signal(barrier, ring(-distance, 1))

    @pl.when(panel == 0)
    def _():
        pl.semaphore_wait(
            barrier, 1 + jnp.where(rad > 0, 2, 0) + jnp.where(rad < n_rad - 1, 2, 0)
        )
        signal(token_sem.at[0], (twin, rad, ang))

    @pl.when(panel == 1)
    def _():
        pl.semaphore_wait(token_sem.at[0], 1)

    def send(src, dst, slot, device):
        return pltpu.make_async_remote_copy(
            src_ref=src,
            dst_ref=dst,
            send_sem=halo_send.at[slot],
            recv_sem=halo_recv.at[slot],
            device_id=device,
            device_id_type=MESH,
        )

    def both(has, pair, act):
        down, up = pair

        @pl.when(has[1])
        def _():
            act(up, down)

        @pl.when(has[0])
        def _():
            act(down, up)

    def start(mine, theirs):
        mine().start()

    def wait_send(mine, theirs):
        mine().wait_send()

    def wait_recv(mine, theirs):
        theirs().wait_recv()

    def rad_copies(g):
        return (
            lambda: send(state_hbm.at[pl.ds(2 * g, 2), pl.ds(0, 3)], halo.at[g, 1], 2 * g, rad_down),
            lambda: send(
                state_hbm.at[pl.ds(2 * g, 2), pl.ds(nr - 3, 3)], halo.at[g, 0], 2 * g + 1, rad_up
            ),
        )

    base = 2 * groups
    rad_vel_copies = (
        lambda: send(velocity_hbm.at[0, 0], halo_vel.at[1], base, rad_down),
        lambda: send(velocity_hbm.at[0, nr - 1], halo_vel.at[0], base + 1, rad_up),
    )
    both(has_rad, rad_vel_copies, start)
    for g in range(groups):
        both(has_rad, rad_copies(g), start)
    @pl.when(panel == 1)
    def _():
        pl.semaphore_wait(barrier, 1 + 4 * reach)
        signal(token_sem.at[1], (twin, rad, ang))

    @pl.when(panel == 0)
    def _():
        pl.semaphore_wait(token_sem.at[1], 1)

    for distance in (-reach, reach):
        signal(token_sem.at[2], ring(distance, panel))

    has_block = (row_index > 0, row_index < n_ang // nr - 1)

    def exchange(source, target, sends, recvs):
        def to(other_row, k, slot, send_slot, recv_slot):
            return pltpu.make_async_remote_copy(
                src_ref=source(k),
                dst_ref=target(slot),
                send_sem=sends.at[send_slot],
                recv_sem=recvs.at[recv_slot],
                device_id=(panel, rad, other_row * nr + k),
                device_id_type=MESH,
            )

        def all_remote(act):
            for step in range(1, nr):
                act(to(row_index, lax.rem(member + step, nr), member + 1, step, 0))

            @pl.when(has_block[1] & (member == nr - 1))
            def _():
                for k in range(nr):
                    act(to(row_index + 1, k, 0, nr + k, 1))

            @pl.when(has_block[0] & (member == 0))
            def _():
                for k in range(nr):
                    act(to(row_index - 1, k, nr + 1, 2 * nr + k, 2))

        def begin():
            all_remote(lambda copy: copy.start())
            pltpu.make_async_copy(source(member), target(member + 1), recvs.at[0]).start()

        def arrive():
            members = target(pl.ds(1, nr))
            pltpu.make_async_copy(members, members, recvs.at[0]).wait()
            for side, slot in ((0, 0), (1, nr + 1)):

                @pl.when(has_block[side])
                def _():
                    edge = target(slot)
                    pltpu.make_async_copy(edge, edge, recvs.at[1 + side]).wait()

        def finish():
            all_remote(lambda copy: copy.wait_send())

        return begin, arrive, finish

    vel_begin, vel_arrive, vel_finish = exchange(
        lambda k: velocity_hbm.at[pl.ds(1, 2), k],
        lambda slot: planes_vel.at[slot],
        plane_send.at[groups],
        plane_recv.at[groups],
    )

    def plane_exchange(g):
        return exchange(
            lambda k: stage.at[g, :, pl.ds(pl.multiple_of(8 * k, 8), 8)],
            lambda slot: planes.at[slot, g],
            plane_send.at[g],
            plane_recv.at[g],
        )

    plane_exchanges = [plane_exchange(g) for g in range(groups)]
    vel_begin()

    load_state.wait()
    load_velocity.wait()
    for g in range(groups):
        for f in range(2):
            for r in range(nr):
                rad_ext[g, 3 + r, f * nt : (f + 1) * nt, :] = own[2 * g + f, r]
    for r in range(nr):
        for f in range(2):
            rad_vel[1 + r, f * nt : (f + 1) * nt, :] = vel[0, r]

    def edges(has, fills):
        for exists, fill in zip(has, fills):
            pl.when(jnp.logical_not(exists))(fill)

    def fill_rad(source, ends, buffers):
        def fill():
            rad_vel[ends[1]] = rad_vel[source]
            for g in range(groups):
                for i in buffers:
                    rad_ext[g, i] = rad_ext[g, source + 2]

        return fill

    edges(
        has_rad,
        (
            fill_rad(1, (1, 0), range(3)),
            fill_rad(nr, (nr, nr + 1), range(nr + 3, nr + 6)),
        ),
    )


    load_donor.wait()
    load_weight.wait()

    donor_all = donor_ref[...]
    donor = jnp.where(panel == 0, donor_all[1:2], donor_all[0:1]).astype(F32)
    donor_row = jnp.floor((donor + 0.5) * (1.0 / nphi))
    donor_col = donor - donor_row * nphi
    weights = jnp.where(panel == 0, weight_ref[1], weight_ref[0])
    row_of = lax.broadcasted_iota(jnp.int32, (row_cells, 128), 0)
    row_of = (row_index * row_cells + row_of).astype(F32)
    col_of = lax.broadcasted_iota(jnp.int32, (nphi, 128), 0).astype(F32)
    for z in range(0, zones, 128):
        here = donor_row[:, z : z + 128]
        w = weights[:, z : z + 128]
        at_row = row_of == here
        above = row_of == here + 1.0
        near_weight[:, z : z + 128] = jnp.where(at_row, w[0:1], jnp.where(above, w[2:3], 0.0))
        far_weight[:, z : z + 128] = jnp.where(at_row, w[1:2], jnp.where(above, w[3:4], 0.0))
        hot = jnp.where(col_of == donor_col[:, z : z + 128], 1.0, 0.0).astype(BF16)
        onehot[0:nphi, z : z + 128] = hot
        onehot[nphi : 2 * nphi, z : z + 128] = hot


    def wide(x, tiles):
        return jnp.concatenate([x] * tiles, axis=-1)


    def lead(n):
        return lax.broadcasted_iota(jnp.int32, (n, 8, 128), 0)


    both(has_rad, rad_vel_copies, wait_recv)
    for side, end in ((0, 0), (1, nr + 1)):

        @pl.when(has_rad[side])
        def _():
            for f in range(2):
                rad_vel[end, f * nt : (f + 1) * nt, :] = halo_vel[side]

    v = rad_vel[...]
    radius_face = INNER_RADIUS + (rad * nr + lead(nr + 1)).astype(F32) * radius_step
    radius_cell = INNER_RADIUS + ((rad * nr + lead(nr)).astype(F32) + 0.5) * radius_step
    rad_coef = flux_coefficients(
        0.5 * (v[0 : nr + 1] + v[1 : nr + 2]),
        wide(radius_face * radius_face, tiles),
        time_step / radius_step,
    )
    rad_rate = wide(time_step / (radius_cell * radius_cell * radius_step), tiles)
    for g in range(groups):
        both(has_rad, rad_copies(g), wait_recv)
        for side, first in ((0, 0), (1, nr + 3)):

            @pl.when(has_rad[side])
            def _():
                for f in range(2):
                    for i in range(3):
                        rad_ext[g, first + i, f * nt : (f + 1) * nt, :] = halo[g, side, f, i]

        after = sweep_leading(rad_ext[g], *rad_coef, rad_rate)
        for r in range(nr):
            put(stage, g, pl.ds(8 * r, 8), after[r])
        plane_exchanges[g][0]()

    vel_arrive()
    for slot in range(nr + 2):
        block_vel[0, slot * nt : (slot + 1) * nt, :] = planes_vel[slot, 0]
    for slot in range(nr):
        block_vel[1, slot * nt : (slot + 1) * nt, :] = planes_vel[slot + 1, 1]
    ext = row_cells + 2 * nt
    ghosts = ((0, nt, nt), (nt + row_cells, ext, nt + row_cells - 1))

    def fill_ghosts(ref, index):
        for side, (first, last, source) in enumerate(ghosts):

            @pl.when(jnp.logical_not(has_block[side]))
            def _():
                for i in index:
                    ref[i, first:last, :] = jnp.broadcast_to(
                        ref[i, source : source + 1, :], (nt, nphi)
                    )

    fill_ghosts(block_vel, range(1))

    def places(n, first):
        return lax.broadcasted_iota(jnp.int32, (n, 128), 0) + (row_index * row_cells + first)

    def shell_radius(n):
        shell = jnp.zeros((n, 128), jnp.int32) + (rad * nr + member)
        return INNER_RADIUS + (shell.astype(F32) + 0.5) * radius_step

    face_place = places(ext, -nt).astype(F32)
    radius = shell_radius(ext)
    u = block_vel[0, 0:ext, :]
    for i, coefficient in enumerate(
        flux_coefficients(
            0.5 * (u + pltpu.roll(u, 1, 0)),
            wide(jnp.sin(theta_start + face_place * theta_step), tiles),
            wide(time_step / (radius * theta_step), tiles),
        )
    ):
        polar_coef[i] = coefficient
    sin_cell = jnp.sin(theta_start + (face_place + 0.5) * theta_step)
    polar_coef[3] = wide(time_step / (radius * sin_cell * theta_step), tiles)
    sin_cell = jnp.sin(theta_start + (places(row_cells, 0).astype(F32) + 0.5) * theta_step)
    rate = wide(time_step / (shell_radius(row_cells) * sin_cell * phi_step), tiles + 1)
    u = with_ghost_lanes(block_vel[1, 0:row_cells, :])
    for i, coefficient in enumerate(
        flux_coefficients(0.5 * (u + pltpu.roll(u, 1, 1)), None, rate)
    ):
        azimuth_coef[i] = coefficient
    azimuth_coef[3] = rate
    pl.semaphore_wait(token_sem.at[2], 2)

    cells = fields * row_cells

    def sweep_field(f):
        q = block[f]
        change = sweep_rolled(q, polar_coef[0], polar_coef[1], polar_coef[2], 0)
        q = (q - polar_coef[3] * change)[nt : nt + row_cells]
        wide_q = with_ghost_lanes(q)
        change = sweep_rolled(wide_q, azimuth_coef[0], azimuth_coef[1], azimuth_coef[2], 1)
        q = (wide_q - azimuth_coef[3] * change)[:, :nphi]
        for k in range(nr):
            for c in range(tiles):
                back_out[k, c, f * nt : (f + 1) * nt, :] = q[
                    k * nt : (k + 1) * nt, 128 * c : 128 * c + 128
                ]
        for i, part in enumerate((q, pltpu.roll(q, nphi - 1, 1))):
            coarse = part.astype(BF16)
            row = i * cells + f * row_cells
            split[row : row + row_cells, 0:nphi] = coarse
            split[row : row + row_cells, nphi : 2 * nphi] = (part - coarse.astype(F32)).astype(BF16)

    for g in range(groups):
        plane_exchanges[g][1]()
        for slot in range(nr + 2):
            for c in range(tiles):
                for f in range(2):
                    block[2 * g + f, slot * nt : (slot + 1) * nt, 128 * c : 128 * c + 128] = planes[
                        slot, g, c, f * nt : (f + 1) * nt, :
                    ]
        fill_ghosts(block, (2 * g, 2 * g + 1))
        for f in range(2):
            sweep_field(2 * g + f)

    def back_copy(step):
        other = lax.rem(member + step, nr)
        return pltpu.make_async_remote_copy(
            src_ref=back_out.at[other],
            dst_ref=result.at[member],
            send_sem=back_send.at[step],
            recv_sem=back_recv,
            device_id=(panel, rad, row_index * nr + other),
            device_id_type=MESH,
        )

    theta_tiles = 2 * G * tiles

    def theta_copy(side):
        return pltpu.make_async_remote_copy(
            src_ref=zone_out.at[pl.ds(side * theta_tiles // 2, theta_tiles // 2)],
            dst_ref=theta_in.at[ang],
            send_sem=zone_send.at[n_ang + side],
            recv_sem=theta_recv,
            device_id=(twin, rad, side * (n_ang - 1)),
            device_id_type=MESH,
        )

    def phi_copy(target):
        return pltpu.make_async_remote_copy(
            src_ref=zone_out.at[theta_tiles + target // (n_ang // 2)],
            dst_ref=phi_in.at[ang],
            send_sem=zone_send.at[target],
            recv_sem=phi_recv,
            device_id=(twin, rad, target),
            device_id_type=MESH,
        )

    def pick(first, last):
        x = split[...]
        for z in range(first, last, 256):
            y = jnp.dot(x, onehot[:, z : z + 256], preferred_element_type=F32)
            near = near_weight[:, z : z + 256].reshape(1, row_cells, 256)
            far = far_weight[:, z : z + 256].reshape(1, row_cells, 256)
            picked = near * y[:cells].reshape(fields, row_cells, 256) + far * y[cells:].reshape(
                fields, row_cells, 256
            )
            picked = picked.reshape(fields, row_cells // 8, 8, 256).sum(axis=1)
            picked = picked.reshape(8 * fields, 256)
            for half in range(2):
                zone_sum[z // 128 + half] = picked[:, 128 * half : 128 * half + 128]
        for z in range(first // 128, last // 128):
            parts = [zone_sum[z, pl.ds(t, fields, stride=8), :] for t in range(8)]
            while len(parts) > 1:
                parts = [a + b for a, b in zip(parts[::2], parts[1::2])]
            zone_out[z, 0:fields, :] = parts[0]

    half_zones = theta_tiles // 2 * 128
    for side in range(2):
        pick(side * half_zones, (side + 1) * half_zones)
        theta_copy(side).start()
    pick(2 * half_zones, zones)
    for target in range(n_ang):
        phi_copy(target).start()
    for step in range(1, nr):
        back_copy(step).start()
    pltpu.make_async_copy(back_out.at[member], result.at[member], back_recv).start()

    pltpu.make_async_copy(result, result, back_recv).wait()
    pltpu.make_async_copy(phi_in, phi_in, phi_recv).wait()
    lane = lax.broadcasted_iota(jnp.int32, (fields, 128), 1)
    first_lane = lax.rem(ang, n_ang // 2) * (2 * G * nt)
    for r in range(nr):
        total = phi_in[r, 0:fields, :]
        for k in range(1, n_ang // nr):
            total = total + phi_in[k * nr + r, 0:fields, :]
        for t in range(nt):
            shift = 256 - first_lane - 2 * G * t
            left = pltpu.roll(total, lax.rem(shift, 128), 1)
            right = pltpu.roll(total, lax.rem(shift - 2 * G, 128), 1)
            rows = pl.ds(t, fields, stride=nt)
            result[r, 0, rows, :] = jnp.where(lane < G, left, result[r, 0, rows, :])
            result[r, tiles - 1, rows, :] = jnp.where(
                lane >= 128 - G, right, result[r, tiles - 1, rows, :]
            )

    def fill_rows(first_row):
        pltpu.make_async_copy(theta_in, theta_in, theta_recv).wait()
        for r in range(nr):
            total = theta_in[r, :, 0:fields, :]
            for k in range(1, n_ang // nr):
                total = total + theta_in[k * nr + r, :, 0:fields, :]
            for row in range(G):
                for c in range(tiles):
                    result[r, c, pl.ds(first_row + row, fields, stride=nt), :] = total[
                        row * tiles + c
                    ]

    @pl.when(ang == 0)
    def _():
        fill_rows(0)

    @pl.when(ang == n_ang - 1)
    def _():
        fill_rows(nt - G)

    for f in range(fields):
        for r in range(nr):
            out_ref[f, r] = jnp.concatenate(
                [result[r, c, f * nt : (f + 1) * nt, :] for c in range(tiles)], axis=1
            )

    both(has_rad, rad_vel_copies, wait_send)
    for g in range(groups):
        both(has_rad, rad_copies(g), wait_send)
    vel_finish()
    for g in range(groups):
        plane_exchanges[g][2]()
    for step in range(1, nr):
        back_copy(step).wait_send()
    for side in range(2):
        theta_copy(side).wait_send()
    for target in range(n_ang):
        phi_copy(target).wait_send()


def solution(mesh):
    n_rad, n_ang = mesh.shape["rad"], mesh.shape["ang"]

    def body(state, velocity, band_donor, band_weight):
        _, fields, nr, nt, nphi = state.shape
        zones = band_donor.shape[1]
        groups = fields // 2
        theta_cells = nt * n_ang
        sizes = (n_rad, n_ang, groups, nr, nt, nphi, theta_cells, zones)
        n_halo = 2 * groups + 2
        tiles, row_cells = nphi // 128, nr * nt
        ext = row_cells + 2 * nt
        out = pl.pallas_call(
            functools.partial(kernel, sizes),
            out_shape=jax.ShapeDtypeStruct((fields, nr, nt, nphi), F32),
            in_specs=[pl.BlockSpec(memory_space=pltpu.HBM)] * 4,
            out_specs=pl.BlockSpec(memory_space=pltpu.VMEM),
            scratch_shapes=[
                pltpu.VMEM((fields, nr, nt, nphi), F32),
                pltpu.VMEM((3, nr, nt, nphi), F32),
                pltpu.VMEM((2, zones), jnp.int32),
                pltpu.VMEM((2, 4, zones), F32),
                pltpu.VMEM((groups, nr + 6, 8, nphi), F32),
                pltpu.VMEM((nr + 2, 8, nphi), F32),
                pltpu.VMEM((groups, 2, 2, 3, nt, nphi), F32),
                pltpu.VMEM((2, nt, nphi), F32),
                pltpu.VMEM((groups, tiles, 8 * nr, 128), F32),
                pltpu.VMEM((nr + 2, groups, tiles, 8, 128), F32),
                pltpu.VMEM((nr + 2, 2, nt, nphi), F32),
                pltpu.VMEM((2, ext, nphi), F32),
                pltpu.VMEM((4, ext, nphi), F32),
                pltpu.VMEM((4, row_cells, nphi + 128), F32),
                pltpu.VMEM((fields, ext, nphi), F32),
                pltpu.VMEM((2 * fields * row_cells, 2 * nphi), BF16),
                pltpu.VMEM((2 * nphi, zones), BF16),
                pltpu.VMEM((row_cells, zones), F32),
                pltpu.VMEM((row_cells, zones), F32),
                pltpu.VMEM((zones // 128, 8 * fields, 128), F32),
                pltpu.VMEM((zones // 128, 8, 128), F32),
                pltpu.VMEM((n_ang, G * tiles, 8, 128), F32),
                pltpu.VMEM((n_ang, 8, 128), F32),
                pltpu.VMEM((nr, tiles, fields * nt, 128), F32),
                pltpu.VMEM((nr, tiles, fields * nt, 128), F32),
                pltpu.SemaphoreType.DMA((4,)),
                pltpu.SemaphoreType.DMA((n_halo,)),
                pltpu.SemaphoreType.DMA((n_halo,)),
                pltpu.SemaphoreType.DMA((groups + 1, 3 * nr)),
                pltpu.SemaphoreType.DMA((groups + 1, 3)),
                pltpu.SemaphoreType.DMA((n_ang + 2,)),
                pltpu.SemaphoreType.DMA,
                pltpu.SemaphoreType.DMA,
                pltpu.SemaphoreType.DMA((nr,)),
                pltpu.SemaphoreType.DMA,
                pltpu.SemaphoreType.REGULAR((3,)),
            ],
            compiler_params=pltpu.CompilerParams(
                collective_id=0, has_side_effects=True, vmem_limit_bytes=40 * 1024 * 1024
            ),
        )(
            *(
                pltpu.with_memory_space_constraint(x, pltpu.HBM)
                for x in (state[0], velocity[0], band_donor, band_weight)
            )
        )
        return out[None]

    spec = P("panel", None, "rad", "ang", None)
    return jax.shard_map(
        body, mesh=mesh, in_specs=(spec, spec, P(), P()), out_specs=spec, check_vma=False
    )
```
